256 devices in a mesh: cam: 2 (over x_lo), band: 32 (over z, y), obj: 4 (over x_hi, core).
Axes of the slice: x: 4 (x_hi: 2, x_lo: 2; x = x_hi * 2 + x_lo), y: 4, z: 8, core: 2. Of those that a mesh axis runs over, the one named last changes fastest.
Arguments:
- queries: bfloat16 [4, 6, 32, 128, 1280], P('obj', 'cam', 'band'), may hold values from -6 to 6
- keys: bfloat16 [4, 6, 32, 128, 1280], P('obj', 'cam', 'band'), may hold values from -6 to 6
- values: bfloat16 [4, 6, 32, 128, 1280], P('obj', 'cam', 'band'), may hold values from -6 to 6
- d_out: bfloat16 [4, 6, 32, 128, 2432], P('obj', 'cam', 'band'), may hold values from -6 to 6
- w_out: bfloat16 [1280, 2432], P(('band', 'obj'), 'cam'), may hold values from -0.15625 to 0.15625
Outputs:
- grad_q: bfloat16 [4, 6, 32, 128, 1280], P('obj', 'cam', 'band')
- grad_k: bfloat16 [4, 6, 32, 128, 1280], P('obj', 'cam', 'band')
- grad_v: bfloat16 [4, 6, 32, 128, 1280], P('obj', 'cam', 'band')
- grad_wo: float32 [1280, 2432], P(('band', 'obj'), 'cam')
The draws below stay inside these ranges and needn't reach their ends.
All inputs are finite; a program needn't handle non-finite values.
Results may differ from the reference program's by a relative error of at most 0.0095.
Values may be sent and summed in bfloat16 or wider, within the bound.
A program may use at most 128 MiB of HBM per device.

```python
import jax
import jax.numpy as jnp
from jax import lax

D = 2432
HEADS = 20
HEAD_DIM = 64
VIEWS = 6
COLS = 128
HD = 1280
ROWS = 32
OBJS = 4
TOKENS = 98304


def draw_queries(key, part):
    shape = (OBJS, VIEWS, ROWS, COLS, HD)
    values = jnp.clip(jax.random.normal(jax.random.fold_in(key, 1), shape, jnp.float32), -6.0, 6.0)
    return values.astype(jnp.bfloat16)


def draw_keys(key, part):
    shape = (OBJS, VIEWS, ROWS, COLS, HD)
    values = jnp.clip(jax.random.normal(jax.random.fold_in(key, 2), shape, jnp.float32), -6.0, 6.0)
    return values.astype(jnp.bfloat16)


def block_scale(rng, extent, cuts, smallest, largest):
    gain = 1.0
    for dim, blocks in cuts:
        draws = jax.random.uniform(jax.random.fold_in(jax.random.fold_in(rng, 6), dim), (blocks,), jnp.float32, smallest / len(cuts), largest / len(cuts))
        gain = gain * jnp.repeat(jnp.exp(draws), extent[dim] // blocks).reshape((-1,) + (1,) * (len(extent) - 1 - dim))
    return gain


def noise(key, extent, spread, reach, pieces=(), dtype=jnp.bfloat16):
    values = jax.random.normal(key, extent, jnp.float32) * spread
    if len(pieces) > 0:
        values = block_scale(key, extent, pieces, -0.22, 0.18) * values
    return jnp.clip(values, min=-reach, max=reach).astype(dtype)


def setup_inputs(seed: int = 0) -> dict:
    key_of = jax.random.split(jax.random.key(seed), 6)
    queries = draw_queries(jax.random.fold_in(key_of[5], 71), 0)
    keys = draw_keys(jax.random.fold_in(key_of[5], 71), 0)
    values = noise(key_of[2], (OBJS, VIEWS, ROWS, COLS, HD), 1.0, 6.0, ((0, 4), (1, 2), (2, 32)))
    d_out = noise(key_of[3], (OBJS, VIEWS, ROWS, COLS, D), 1.0, 6.0, ((0, 4), (1, 2), (2, 32)))
    w_out = noise(key_of[4], (HD, D), HD ** -0.5, 0.15625, ((0, 128), (1, 2)))
    return {"queries": queries, "keys": keys, "values": values, "d_out": d_out, "w_out": w_out}


def rounded(x):
    return lax.optimization_barrier(x.astype(jnp.bfloat16)).astype(jnp.float32)


def group_backward(parts):
    q_group, k_group, v_group, d_group = parts
    qf = q_group.astype(jnp.float32)
    kf = k_group.astype(jnp.float32)
    vf = v_group.astype(jnp.float32)
    df = d_group.astype(jnp.float32)
    scores = jnp.einsum("qhe,khe->hqk", qf, kf) * 0.125
    top = jnp.max(scores, axis=-1, keepdims=True)
    expd = jnp.exp(scores - top)
    probs = expd / jnp.sum(expd, axis=-1, keepdims=True)
    probs_b = rounded(probs)
    att = jnp.einsum("hqk,khe->qhe", probs_b, vf).astype(jnp.bfloat16)
    d_probs = jnp.einsum("qhe,khe->hqk", df, vf)
    delta = jnp.sum(probs * d_probs, axis=-1, keepdims=True)
    d_scores_b = rounded(probs * (d_probs - delta))
    grad_q = (jnp.einsum("hqk,khe->qhe", d_scores_b, kf) * 0.125).astype(jnp.bfloat16)
    grad_k = (jnp.einsum("hqk,qhe->khe", d_scores_b, qf) * 0.125).astype(jnp.bfloat16)
    grad_v = jnp.einsum("hqk,qhe->khe", probs_b, df).astype(jnp.bfloat16)
    return grad_q, grad_k, grad_v, att


def to_groups(x):
    return x.transpose(0, 2, 1, 3, 4).reshape(OBJS * ROWS, VIEWS * COLS, HEADS, HEAD_DIM)


def from_groups(x):
    return x.reshape(OBJS, ROWS, VIEWS, COLS, HD).transpose(0, 2, 1, 3, 4)


def reference(queries, keys, values, d_out, w_out):
    flat_out = d_out.reshape(TOKENS, D)
    d_att = jnp.dot(flat_out, w_out.T, preferred_element_type=jnp.float32).astype(jnp.bfloat16)
    d_att = d_att.reshape(OBJS, VIEWS, ROWS, COLS, HD)
    results = lax.map(group_backward, (to_groups(queries), to_groups(keys), to_groups(values), to_groups(d_att)))
    grad_q, grad_k, grad_v, att = [from_groups(r) for r in results]
    flat_att = att.reshape(TOKENS, HD)
    grad_wo = jnp.dot(flat_att.T, flat_out, preferred_element_type=jnp.float32)
    grad_wo = grad_wo * (jnp.float32(TOKENS) ** -0.5)
    return grad_q, grad_k, grad_v, grad_wo
```

```python
import functools
import math

import jax
import jax.numpy as jnp
from jax import lax
from jax.experimental import pallas as pl
from jax.experimental.pallas import tpu as pltpu
from jax.sharding import PartitionSpec as P

BF = jnp.bfloat16
F32 = jnp.float32
MESH = pl.DeviceIdType.MESH
NY, NZ = 4, 8
RING = NZ - 1
LAG = 10
RING_AT = 0
EXP_SCALE = 0.125 / math.log(2.0)


def nn(a, b):
    return lax.dot_general(a, b, (((1,), (0,)), ((), ())), preferred_element_type=F32)


def nt(a, b):
    return lax.dot_general(a, b, (((1,), (1,)), ((), ())), preferred_element_type=F32)


def picker(rows, cols, row_step, col_step, width):
    r = lax.broadcasted_iota(jnp.int32, (rows, cols), 0)
    c = lax.broadcasted_iota(jnp.int32, (rows, cols), 1)
    pick = jnp.zeros((rows, cols), F32)
    for b in range(4):
        k = r - row_step * b
        hit = (k >= 0) & (k < width) & (c - col_step * b == k)
        pick = pick + jnp.where(hit, 1.0, 0.0).astype(F32)
    return pick.astype(BF)


def halves(x, axis):
    index = lax.broadcasted_iota(jnp.int32, x.shape, axis)
    first = jnp.where(index < x.shape[axis] // 2, x, 0.0)
    return first.astype(BF), (x - first).astype(BF)


def kernel(scale, q_hbm, k_hbm, v_hbm, d_hbm, w_ref, gq_hbm, gk_hbm, gv_hbm, gwo_ref,
           qb, kb, vb, dfull, dcat, doth, wpad, wx, wy, wown, woth, att, lse, osum,
           dks, dkr, dko, gq_st, gk_st, gv_st, gacc, rss, rsr, gys, gyr, gxs, gxr,
           q_ld, k_ld, v_ld, d_ld, wx_s, wx_r, wy_s, wy_r, zr_s, zr_r, zl_s, zl_r,
           oc_s, oc_r, k_s, k_r, v_s, v_r, dx_s, dx_r, at_s, at_r, dk_s, dk_r, dv_s, dv_r,
           rr_s, rr_r, rl_s, rl_r, gy_s, gy_r, gx_s, gx_r, gq_o, gk_o, gv_o):
    pairs, toks = qb.shape[0], qb.shape[1]
    cols = wpad.shape[1]
    blk = wown.shape[0] // NZ
    half = blk // 2
    cam, band, obj = lax.axis_index("cam"), lax.axis_index("band"), lax.axis_index("obj")
    z, y = band // NY, band % NY
    xh, core = obj // 2, obj % 2
    x = xh * 2 + cam
    base = (blk * z + half) // 128

    def dev(cam_=None, band_=None, obj_=None):
        return {
            "cam": cam if cam_ is None else cam_,
            "band": band if band_ is None else band_,
            "obj": obj if obj_ is None else obj_,
        }

    def at_z(shift):
        return dev(band_=lax.rem(z + shift + NZ, NZ) * NY + y)

    def at_y(shift):
        return dev(band_=z * NY + lax.rem(y + shift, NY))

    cam_peer = dev(cam_=1 - cam)
    core_peer = dev(obj_=xh * 2 + 1 - core)
    z_up, z_down = at_z(1), at_z(-1)

    def remote(src, dst, send, recv, device):
        return pltpu.make_async_remote_copy(
            src_ref=src, dst_ref=dst, send_sem=send, recv_sem=recv, device_id=device,
            device_id_type=MESH)

    def order(i):
        step = (i + 1) // 2
        sign = 2 * (i % 2) - 1
        return lax.rem(base + sign * step + pairs, pairs)

    def lanes(i):
        return pl.ds(pl.multiple_of(order(i) * 128, 128), 128)

    def load_q(i):
        return pltpu.make_async_copy(q_hbm.at[:, lanes(i)], qb.at[i], q_ld.at[i])

    def load_k(i):
        return pltpu.make_async_copy(k_hbm.at[:, lanes(i)], kb.at[i, 0], k_ld.at[i])

    def load_v(i):
        return pltpu.make_async_copy(v_hbm.at[:, lanes(i)], vb.at[i, 0], v_ld.at[i])

    def send_k(i):
        return remote(k_hbm.at[:, lanes(i)], kb.at[i, 1], k_s.at[i], k_r.at[i], cam_peer)

    def send_v(i):
        return remote(v_hbm.at[:, lanes(i)], vb.at[i, 1], v_s.at[i], v_r.at[i], cam_peer)

    load_d = pltpu.make_async_copy(d_hbm, dfull, d_ld)
    load_d.start()
    wpad[...] = jnp.zeros_like(wpad)
    wpad[0:10, :] = w_ref[...]

    @pl.loop(0, pairs)
    def _(i):
        load_q(i).start()
        load_k(i).start()
        load_v(i).start()

    barrier = pltpu.get_barrier_semaphore()
    peers = [dev(cam_=lax.rem(cam + a, 2), obj_=lax.rem(obj + b, 4))
             for a in range(2) for b in range(4) if a + b > 0]
    peers += [at_y(s) for s in range(1, NY)] + [z_up, z_down]
    for peer in peers:
        pl.semaphore_signal(barrier, inc=1, device_id=peer, device_id_type=MESH)
    pl.semaphore_wait(barrier, len(peers))

    def w_to(t):
        return remote(wpad, wx.at[obj], wx_s.at[t], wx_r.at[obj],
                      dev(cam_=t % 2, obj_=(t // 2) * 2 + cam))

    own_target = core == cam
    for t in range(4):
        mine = own_target & (x == t)

        @pl.when(jnp.logical_not(mine))
        def _():
            w_to(t).start()

    @pl.when(own_target)
    def _():
        pltpu.make_async_copy(wpad, wx.at[obj], wx_r.at[obj]).start()

    @pl.loop(0, pairs)
    def _(i):
        send_k(i).start()
        send_v(i).start()

    load_d.wait()
    low, high = dfull[:, 0:cols], dfull[:, cols:2 * cols]

    @pl.when(core == 0)
    def _():
        dcat[0:toks, :] = low
        doth[...] = high

    @pl.when(core == 1)
    def _():
        dcat[0:toks, :] = high
        doth[...] = low

    d_swap = remote(doth, dcat.at[pl.ds(toks, toks)], dx_s, dx_r, core_peer)
    d_swap.start()

    for o in range(4):
        pltpu.make_async_copy(wpad, wx.at[o], wx_r.at[o]).wait()
    joined = nn(picker(48, 64, 10, 16, 10), wx[...].reshape(64, cols)).astype(BF)
    wy[y] = joined

    def y_copy(s):
        return remote(wy.at[y], wy.at[y], wy_s.at[s], wy_r.at[s], at_y(s))

    for s in range(1, NY):
        y_copy(s).start()
    for s in range(1, NY):
        y_copy(s).wait_recv()

    def block_rows(b, size=None, off=0):
        return pl.ds(pl.multiple_of(b * blk + off, 16), blk if size is None else size)

    wown[block_rows(z), :] = nn(picker(blk, 4 * 48, 40, 48, 40), wy[...].reshape(4 * 48, cols)).astype(BF)

    def up_copy(h, back):
        b = lax.rem(z - h // 2 - back + NZ, NZ)
        rows = block_rows(b, half, (h % 2) * half)
        return remote(wown.at[rows], wown.at[rows], zr_s.at[h], zr_r.at[h], z_up)

    def down_copy(h, back):
        b = lax.rem(z + h // 2 + back, NZ)
        rows = block_rows(b, half, (1 - h % 2) * half)
        return remote(wown.at[rows], wown.at[rows], zl_s.at[h], zl_r.at[h], z_down)

    def cross(h, up):
        b = lax.rem(z - h // 2 - 1 + NZ, NZ) if up else lax.rem(z + h // 2 + 1, NZ)
        j = h % 2 if up else 1 - h % 2
        rows = block_rows(b, half, j * half)
        n = 2 * h + (0 if up else 1)
        return remote(wown.at[rows], woth.at[rows], oc_s.at[n], oc_r.at[n], core_peer)

    own_rows = block_rows(z)
    cross_own = remote(wown.at[own_rows], woth.at[own_rows], oc_s.at[2 * RING], oc_r.at[2 * RING], core_peer)
    for h in range(2):
        up_copy(h, 0).start()
        down_copy(h, 0).start()
    cross_own.start()

    def ring(h):
        up_copy(h, 1).wait_recv()

        @pl.when(h + 2 < RING)
        def _():
            up_copy(h + 2, 0).start()

        down_copy(h, 1).wait_recv()

        @pl.when(h + 2 < RING)
        def _():
            down_copy(h + 2, 0).start()

        cross(h, True).start()
        cross(h, False).start()

    def split_q(i):
        first, second = halves(qb[i].astype(F32), 1)
        return jnp.concatenate([first, second], axis=0)

    def swap_att(i):
        rows = pl.ds(pl.multiple_of(order(i) * 128, 128), 128)
        return remote(att.at[rows, pl.ds(0, toks)], att.at[rows, pl.ds(toks, toks)],
                      at_s.at[i], at_r.at[i], core_peer)

    part = 2 * toks // 3

    def forward(i):
        load_q(i).wait()
        load_k(i).wait()
        load_v(i).wait()
        send_k(i).wait_recv()
        send_v(i).wait_recv()
        kk = kb[i].reshape(2 * toks, 128)
        vt = vb[i].reshape(2 * toks, 128).T
        qm = split_q(i)
        for n in range(3):
            s = nt(kk, qm[n * part:(n + 1) * part])
            top = jnp.max(s, axis=0, keepdims=True)
            e = jnp.exp2((s - top) * EXP_SCALE)
            total = jnp.sum(e, axis=0, keepdims=True)
            osum[:, n * part:(n + 1) * part] = nn(vt, e.astype(BF)) * (1.0 / total)
            lse[i, :, n * part:(n + 1) * part] = top * EXP_SCALE + jnp.log2(total)
        rows = pl.ds(pl.multiple_of(order(i) * 128, 128), 128)
        both = jnp.concatenate([osum[0:64, 0:toks], osum[64:128, toks:2 * toks]], axis=0)
        att[rows, 0:toks] = both.astype(BF)
        swap_att(i).start()

    def give_k(i):
        return remote(dks.at[i, 0], dkr.at[i, 0], dk_s.at[i], dk_r.at[i], cam_peer)

    def give_v(i):
        return remote(dks.at[i, 1], dkr.at[i, 1], dv_s.at[i], dv_r.at[i], cam_peer)

    def put_q(i):
        return pltpu.make_async_copy(gq_st.at[i], gq_hbm.at[:, lanes(i)], gq_o.at[i])

    def put_k(i):
        return pltpu.make_async_copy(gk_st.at[i], gk_hbm.at[:, lanes(i)], gk_o.at[i])

    def put_v(i):
        return pltpu.make_async_copy(gv_st.at[i], gv_hbm.at[:, lanes(i)], gv_o.at[i])

    def backward(i):
        rows = pl.ds(pl.multiple_of(order(i) * 128, 128), 128)
        da = nt(wown[rows, :], dcat[0:toks, :]) + nt(woth[rows, :], doth[...])
        da = da.astype(BF).astype(F32)
        prod = da * att[rows, 0:toks].astype(F32)
        delta = jnp.concatenate([jnp.sum(prod[0:64], axis=0, keepdims=True),
                                 jnp.sum(prod[64:128], axis=0, keepdims=True)], axis=1)
        dm = jnp.concatenate(halves(da, 0), axis=1)
        kk = kb[i].reshape(2 * toks, 128)
        vv = vb[i].reshape(2 * toks, 128)
        kt = kk.T
        qm = split_q(i)
        dk = dv = None
        for n in range(3):
            at = slice(n * part, (n + 1) * part)
            s = nt(kk, qm[at])
            p = jnp.exp2(s * EXP_SCALE - lse[i, :, at])
            dp = nn(vv, dm[:, at])
            ds = (p * (dp - delta[:, at])).astype(BF)
            dv_n = nt(p.astype(BF), dm[:, at])
            dk_n = nn(ds, qm[at])
            dv = dv_n if dv is None else dv + dv_n
            dk = dk_n if dk is None else dk + dk_n
            osum[:, at] = nn(kt, ds)
        dk = dk * 0.125
        dks[i, 0] = dk[toks:].astype(BF)
        dks[i, 1] = dv[toks:].astype(BF)
        give_k(i).start()
        give_v(i).start()
        dko[i, 0] = dk[:toks]
        dko[i, 1] = dv[:toks]
        both = jnp.concatenate([osum[0:64, 0:toks], osum[64:128, toks:2 * toks]], axis=0)
        gq_st[i] = (both.T * 0.125).astype(BF)
        put_q(i).start()

    def finish(i):
        give_k(i).wait_recv()
        gk_st[i] = (dko[i, 0] + dkr[i, 0].astype(F32)).astype(BF)
        put_k(i).start()
        give_v(i).wait_recv()
        gv_st[i] = (dko[i, 1] + dkr[i, 1].astype(F32)).astype(BF)
        put_v(i).start()

    def sum_up(s):
        return remote(rss.at[s, 0], rsr.at[s, 0], rr_s.at[s], rr_r.at[s], z_up)

    def sum_down(s):
        return remote(rss.at[s, 1], rsr.at[s, 1], rl_s.at[s], rl_r.at[s], z_down)

    def sum_step(s):
        owner_up = lax.rem(z - 1 - s + 2 * NZ, NZ)
        owner_down = lax.rem(z + 1 + s, NZ)
        rows = jnp.concatenate([att[block_rows(owner_up, half), :],
                                att[block_rows(owner_down, half, half), :]], axis=0)
        gacc[...] = nn(rows, dcat[...])

        @pl.when(s > 0)
        def _():
            sum_up(s - 1).wait_recv()
            gacc[0:half, :] = gacc[0:half, :] + rsr[s - 1, 0].astype(F32)
            sum_down(s - 1).wait_recv()
            gacc[half:blk, :] = gacc[half:blk, :] + rsr[s - 1, 1].astype(F32)

        @pl.when(s < RING)
        def _():
            rss[s, 0] = gacc[0:half, :].astype(BF)
            sum_up(s).start()
            rss[s, 1] = gacc[half:blk, :].astype(BF)
            sum_down(s).start()

    @pl.loop(0, pairs + LAG)
    def _(t):
        h = t - RING_AT

        @pl.when((h >= 0) & (h < RING))
        def _():
            ring(h)

        @pl.when(t < pairs)
        def _():
            forward(t)

        @pl.when(t == pairs - 1)
        def _():
            d_swap.wait_recv()
            cross_own.wait_recv()
            for n in range(RING):
                cross(n, True).wait_recv()
                cross(n, False).wait_recv()

            @pl.loop(0, pairs)
            def _(i):
                swap_att(i).wait_recv()

        @pl.when(t >= LAG)
        def _():
            backward(t - LAG)

        s = t - pairs

        @pl.when((s >= 0) & (s < NZ))
        def _():
            sum_step(s)

    def sum_y(s):
        return remote(gys.at[lax.rem(y + s, NY)], gyr.at[s], gy_s.at[s], gy_r.at[s], at_y(s))

    gys[...] = nn(picker(4 * 48, blk, 48, 40, 40), gacc[...].astype(BF)).astype(BF).reshape(4, 48, cols)
    for s in range(1, NY):
        sum_y(s).start()
    summed = gys[y].astype(F32)
    for s in range(1, NY):
        sum_y(s).wait_recv()
        summed = summed + gyr[s].astype(F32)
    gxs[...] = nn(picker(64, 48, 16, 10, 10), summed.astype(BF)).astype(BF).reshape(4, 16, cols)

    def sum_x(o):
        return remote(gxs.at[o], gxr.at[x], gx_s.at[o], gx_r.at[x], dev(cam_=core, obj_=o))

    for o in range(4):
        mine = own_target & (obj == o)

        @pl.when(jnp.logical_not(mine))
        def _():
            sum_x(o).start()

        @pl.when(mine)
        def _():
            pltpu.make_async_copy(gxs.at[o], gxr.at[x], gx_r.at[x]).start()

    @pl.loop(0, pairs)
    def _(i):
        finish(i)

    for o in range(4):
        pltpu.make_async_copy(gxs.at[o], gxr.at[o], gx_r.at[o]).wait()
    total = gxr[0].astype(F32) + gxr[1].astype(F32) + gxr[2].astype(F32) + gxr[3].astype(F32)
    gwo_ref[...] = total[0:10, :] * scale

    for t in range(4):
        @pl.when(jnp.logical_not(own_target & (x == t)))
        def _():
            w_to(t).wait_send()

        @pl.when(jnp.logical_not(own_target & (obj == t)))
        def _():
            sum_x(t).wait_send()

    for s in range(1, NY):
        y_copy(s).wait_send()
        sum_y(s).wait_send()
    d_swap.wait_send()
    cross_own.wait_send()

    @pl.loop(0, RING)
    def _(h):
        up_copy(h, 0).wait_send()
        down_copy(h, 0).wait_send()
        cross(h, True).wait_send()
        cross(h, False).wait_send()
        sum_up(h).wait_send()
        sum_down(h).wait_send()

    @pl.loop(0, pairs)
    def _(i):
        send_k(i).wait_send()
        send_v(i).wait_send()
        swap_att(i).wait_send()
        give_k(i).wait_send()
        give_v(i).wait_send()
        put_q(i).wait()
        put_k(i).wait()
        put_v(i).wait()


def body(queries, keys, values, d_out, w_out):
    shape = queries.shape
    width, model = queries.shape[4], d_out.shape[4]
    toks = queries.shape[1] * queries.shape[2] * queries.shape[3]
    tokens = toks * lax.axis_size("cam") * lax.axis_size("band") * lax.axis_size("obj")
    scale = float(tokens) ** -0.5
    pairs = width // 128
    cols = w_out.shape[1]
    blk = width // NZ
    dma = lambda *n: pltpu.SemaphoreType.DMA(n)
    flat = lambda a: a.reshape(toks, a.shape[4])
    any_ = pl.BlockSpec(memory_space=pl.ANY)
    vmem = pl.BlockSpec(memory_space=pltpu.VMEM)
    grad = jax.ShapeDtypeStruct((toks, width), BF)
    scratch = [
        pltpu.VMEM((pairs, toks, 128), BF),
        pltpu.VMEM((pairs, 2, toks, 128), BF),
        pltpu.VMEM((pairs, 2, toks, 128), BF),
        pltpu.VMEM((toks, model), BF),
        pltpu.VMEM((2 * toks, cols), BF),
        pltpu.VMEM((toks, cols), BF),
        pltpu.VMEM((16, cols), BF),
        pltpu.VMEM((4, 16, cols), BF),
        pltpu.VMEM((4, 48, cols), BF),
        pltpu.VMEM((width, cols), BF),
        pltpu.VMEM((width, cols), BF),
        pltpu.VMEM((width, 2 * toks), BF),
        pltpu.VMEM((pairs, 1, 2 * toks), F32),
        pltpu.VMEM((128, 2 * toks), F32),
        pltpu.VMEM((pairs, 2, toks, 128), BF),
        pltpu.VMEM((pairs, 2, toks, 128), BF),
        pltpu.VMEM((pairs, 2, toks, 128), F32),
        pltpu.VMEM((pairs, toks, 128), BF),
        pltpu.VMEM((pairs, toks, 128), BF),
        pltpu.VMEM((pairs, toks, 128), BF),
        pltpu.VMEM((blk, cols), F32),
        pltpu.VMEM((RING, 2, blk // 2, cols), BF),
        pltpu.VMEM((RING, 2, blk // 2, cols), BF),
        pltpu.VMEM((4, 48, cols), BF),
        pltpu.VMEM((4, 48, cols), BF),
        pltpu.VMEM((4, 16, cols), BF),
        pltpu.VMEM((4, 16, cols), BF),
        dma(pairs), dma(pairs), dma(pairs), pltpu.SemaphoreType.DMA,
        dma(4), dma(4), dma(4), dma(4), dma(RING), dma(RING), dma(RING), dma(RING),
        dma(2 * RING + 1), dma(2 * RING + 1), dma(pairs), dma(pairs), dma(pairs), dma(pairs),
        pltpu.SemaphoreType.DMA, pltpu.SemaphoreType.DMA, dma(pairs), dma(pairs),
        dma(pairs), dma(pairs), dma(pairs), dma(pairs),
        dma(RING), dma(RING), dma(RING), dma(RING), dma(4), dma(4), dma(4), dma(4),
        dma(pairs), dma(pairs), dma(pairs),
    ]
    gq, gk, gv, gwo = pl.pallas_call(
        functools.partial(kernel, scale),
        out_shape=(grad, grad, grad, jax.ShapeDtypeStruct(w_out.shape, F32)),
        in_specs=[any_] * 4 + [vmem],
        out_specs=(any_, any_, any_, vmem),
        scratch_shapes=scratch,
        compiler_params=pltpu.CompilerParams(
            collective_id=0, has_side_effects=True, vmem_limit_bytes=64 * 1024 * 1024 - 65536),
        name="row_attention_backward",
    )(flat(queries), flat(keys), flat(values), flat(d_out), w_out)
    return gq.reshape(shape), gk.reshape(shape), gv.reshape(shape), gwo


def solution(mesh):
    act = P("obj", "cam", "band", None, None)
    proj = P(("band", "obj"), "cam")
    return jax.shard_map(
        body,
        mesh=mesh,
        in_specs=(act, act, act, act, proj),
        out_specs=(act, act, act, proj),
        check_vma=False,
    )
```

```python
import functools
import math

import jax
import jax.numpy as jnp
from jax import lax
from jax.experimental import pallas as pl
from jax.experimental.pallas import tpu as pltpu
from jax.sharding import PartitionSpec as P

BF = jnp.bfloat16
F32 = jnp.float32
MESH = pl.DeviceIdType.MESH
NY, NZ = 4, 8
RING = NZ - 1
LAG = 6
RING_AT = 4
SUBS = ((0, 48), (48, 32))
EXP_SCALE = 0.125 / math.log(2.0)


def nn(a, b):
    return lax.dot_general(a, b, (((1,), (0,)), ((), ())), preferred_element_type=F32)


def nt(a, b):
    return lax.dot_general(a, b, (((1,), (1,)), ((), ())), preferred_element_type=F32)


def picker(rows, cols, row_step, col_step, width):
    r = lax.broadcasted_iota(jnp.int32, (rows, cols), 0)
    c = lax.broadcasted_iota(jnp.int32, (rows, cols), 1)
    pick = jnp.zeros((rows, cols), F32)
    for b in range(4):
        k = r - row_step * b
        hit = (k >= 0) & (k < width) & (c - col_step * b == k)
        pick = pick + jnp.where(hit, 1.0, 0.0).astype(F32)
    return pick.astype(BF)


def halves(x, axis):
    index = lax.broadcasted_iota(jnp.int32, x.shape, axis)
    first = jnp.where(index < x.shape[axis] // 2, x, 0.0)
    return first.astype(BF), (x - first).astype(BF)


def kernel(scale, q_hbm, k_hbm, v_hbm, d_hbm, w_ref, gq_hbm, gk_hbm, gv_hbm, gwo_ref,
           qb, kb, vb, dfull, dcat, doth, wpad, wx, wy, wown, woth, att, lse, osum,
           dks, dkr, dko, gq_st, gk_st, gv_st, gacc, rss, rsr, gys, gyr, gxs, gxr,
           q_ld, k_ld, v_ld, d_ld, wx_s, wx_r, wy_s, wy_r, zr_s, zr_r, zl_s, zl_r,
           oc_s, oc_r, k_s, k_r, v_s, v_r, dx_s, dx_r, at_s, at_r, dk_s, dk_r, dv_s, dv_r,
           rr_s, rr_r, rl_s, rl_r, gy_s, gy_r, gx_s, gx_r, gq_o, gk_o, gv_o):
    pairs, toks = qb.shape[0], qb.shape[1]
    cols = wpad.shape[1]
    blk = wown.shape[0] // NZ
    half = blk // 2
    cam, band, obj = lax.axis_index("cam"), lax.axis_index("band"), lax.axis_index("obj")
    z, y = band // NY, band % NY
    xh, core = obj // 2, obj % 2
    x = xh * 2 + cam
    base = (blk * z + half) // 128

    def dev(cam_=None, band_=None, obj_=None):
        return {
            "cam": cam if cam_ is None else cam_,
            "band": band if band_ is None else band_,
            "obj": obj if obj_ is None else obj_,
        }

    def at_z(shift):
        return dev(band_=lax.rem(z + shift + NZ, NZ) * NY + y)

    def at_y(shift):
        return dev(band_=z * NY + lax.rem(y + shift, NY))

    cam_peer = dev(cam_=1 - cam)
    core_peer = dev(obj_=xh * 2 + 1 - core)
    z_up, z_down = at_z(1), at_z(-1)

    def remote(src, dst, send, recv, device):
        return pltpu.make_async_remote_copy(
            src_ref=src, dst_ref=dst, send_sem=send, recv_sem=recv, device_id=device,
            device_id_type=MESH)

    def order(i):
        step = (i + 1) // 2
        sign = 2 * (i % 2) - 1
        return lax.rem(base + sign * step + pairs, pairs)

    def lanes(i):
        return pl.ds(pl.multiple_of(order(i) * 128, 128), 128)

    def load_q(i):
        return pltpu.make_async_copy(q_hbm.at[:, lanes(i)], qb.at[i], q_ld.at[i])

    def load_k(i):
        return pltpu.make_async_copy(k_hbm.at[:, lanes(i)], kb.at[i, 0], k_ld.at[i])

    def load_v(i):
        return pltpu.make_async_copy(v_hbm.at[:, lanes(i)], vb.at[i, 0], v_ld.at[i])

    def send_k(i):
        return remote(k_hbm.at[:, lanes(i)], kb.at[i, 1], k_s.at[i], k_r.at[i], cam_peer)

    def send_v(i):
        return remote(v_hbm.at[:, lanes(i)], vb.at[i, 1], v_s.at[i], v_r.at[i], cam_peer)

    load_d = pltpu.make_async_copy(d_hbm, dfull, d_ld)
    load_d.start()
    wpad[...] = jnp.zeros_like(wpad)
    wpad[0:10, :] = w_ref[...]

    @pl.loop(0, pairs)
    def _(i):
        load_q(i).start()
        load_k(i).start()
        load_v(i).start()

    barrier = pltpu.get_barrier_semaphore()
    peers = [dev(cam_=lax.rem(cam + a, 2), obj_=lax.rem(obj + b, 4))
             for a in range(2) for b in range(4) if a + b > 0]
    peers += [at_y(s) for s in range(1, NY)] + [z_up, z_down]
    for peer in peers:
        pl.semaphore_signal(barrier, inc=1, device_id=peer, device_id_type=MESH)
    pl.semaphore_wait(barrier, len(peers))

    def w_to(t):
        return remote(wpad, wx.at[obj], wx_s.at[t], wx_r.at[obj],
                      dev(cam_=t % 2, obj_=(t // 2) * 2 + cam))

    own_target = core == cam
    for t in range(4):
        mine = own_target & (x == t)

        @pl.when(jnp.logical_not(mine))
        def _():
            w_to(t).start()

    @pl.when(own_target)
    def _():
        pltpu.make_async_copy(wpad, wx.at[obj], wx_r.at[obj]).start()

    @pl.loop(0, pairs)
    def _(i):
        send_k(i).start()
        send_v(i).start()

    join_x = picker(48, 64, 10, 16, 10)
    for o in range(4):
        pltpu.make_async_copy(wpad, wx.at[o], wx_r.at[o]).wait()
    joined = nn(join_x, wx[...].reshape(64, cols)).astype(BF)
    wy[y] = joined

    def y_copy(s):
        return remote(wy.at[y], wy.at[y], wy_s.at[s], wy_r.at[s], at_y(s))

    for s in range(1, NY):
        y_copy(s).start()

    load_d.wait()
    low, high = dfull[:, 0:cols], dfull[:, cols:2 * cols]

    @pl.when(core == 0)
    def _():
        dcat[0:toks, :] = low
        doth[...] = high

    @pl.when(core == 1)
    def _():
        dcat[0:toks, :] = high
        doth[...] = low

    d_swap = remote(doth, dcat.at[pl.ds(toks, toks)], dx_s, dx_r, core_peer)
    d_swap.start()

    join_y = picker(blk, 4 * 48, 40, 48, 40)
    for s in range(1, NY):
        y_copy(s).wait_recv()

    def block_rows(b, size=None, off=0):
        return pl.ds(pl.multiple_of(b * blk + off, 16), blk if size is None else size)

    wown[block_rows(z), :] = nn(join_y, wy[...].reshape(4 * 48, cols)).astype(BF)

    def up_copy(h, back):
        b = lax.rem(z - h // 2 - back + NZ, NZ)
        rows = block_rows(b, half, (h % 2) * half)
        return remote(wown.at[rows], wown.at[rows], zr_s.at[h], zr_r.at[h], z_up)

    def down_copy(h, back):
        b = lax.rem(z + h // 2 + back, NZ)
        rows = block_rows(b, half, (1 - h % 2) * half)
        return remote(wown.at[rows], wown.at[rows], zl_s.at[h], zl_r.at[h], z_down)

    def cross(h, up):
        b = lax.rem(z - h // 2 - 1 + NZ, NZ) if up else lax.rem(z + h // 2 + 1, NZ)
        j = h % 2 if up else 1 - h % 2
        rows = block_rows(b, half, j * half)
        n = 2 * h + (0 if up else 1)
        return remote(wown.at[rows], woth.at[rows], oc_s.at[n], oc_r.at[n], core_peer)

    own_rows = block_rows(z)
    cross_own = remote(wown.at[own_rows], woth.at[own_rows], oc_s.at[2 * RING], oc_r.at[2 * RING], core_peer)
    for h in range(2):
        up_copy(h, 0).start()
        down_copy(h, 0).start()
    cross_own.start()

    def ring(h):
        up_copy(h, 1).wait_recv()

        @pl.when(h + 2 < RING)
        def _():
            up_copy(h + 2, 0).start()

        down_copy(h, 1).wait_recv()

        @pl.when(h + 2 < RING)
        def _():
            down_copy(h + 2, 0).start()

        cross(h, True).start()
        cross(h, False).start()

    def split_q(i):
        first, second = halves(qb[i].astype(F32), 1)
        return jnp.concatenate([first, second], axis=0)

    def swap_att(i):
        rows = pl.ds(pl.multiple_of(order(i) * 128, 128), 128)
        return remote(att.at[rows, pl.ds(0, toks)], att.at[rows, pl.ds(toks, toks)],
                      at_s.at[i], at_r.at[i], core_peer)

    part = 2 * toks // 3

    def forward(i):
        load_q(i).wait()
        load_k(i).wait()
        load_v(i).wait()
        send_k(i).wait_recv()
        send_v(i).wait_recv()
        kk = kb[i].reshape(2 * toks, 128)
        vt = vb[i].reshape(2 * toks, 128).T
        qm = split_q(i)
        for n in range(3):
            s = nt(kk, qm[n * part:(n + 1) * part])
            top = jnp.max(s, axis=0, keepdims=True)
            e = jnp.exp2((s - top) * EXP_SCALE)
            total = jnp.sum(e, axis=0, keepdims=True)
            osum[:, n * part:(n + 1) * part] = nn(vt, e.astype(BF)) * (1.0 / total)
            lse[i, :, n * part:(n + 1) * part] = top * EXP_SCALE + jnp.log2(total)
        rows = pl.ds(pl.multiple_of(order(i) * 128, 128), 128)
        both = jnp.concatenate([osum[0:64, 0:toks], osum[64:128, toks:2 * toks]], axis=0)
        att[rows, 0:toks] = both.astype(BF)
        swap_att(i).start()

    def give_k(i):
        return remote(dks.at[i, 0], dkr.at[i, 0], dk_s.at[i], dk_r.at[i], cam_peer)

    def give_v(i):
        return remote(dks.at[i, 1], dkr.at[i, 1], dv_s.at[i], dv_r.at[i], cam_peer)

    def put_q(i):
        return pltpu.make_async_copy(gq_st.at[i], gq_hbm.at[:, lanes(i)], gq_o.at[i])

    def put_k(i):
        return pltpu.make_async_copy(gk_st.at[i], gk_hbm.at[:, lanes(i)], gk_o.at[i])

    def put_v(i):
        return pltpu.make_async_copy(gv_st.at[i], gv_hbm.at[:, lanes(i)], gv_o.at[i])

    def backward(i):
        rows = pl.ds(pl.multiple_of(order(i) * 128, 128), 128)
        da = nt(wown[rows, :], dcat[0:toks, :]) + nt(woth[rows, :], doth[...])
        da = da.astype(BF).astype(F32)
        prod = da * att[rows, 0:toks].astype(F32)
        delta = jnp.concatenate([jnp.sum(prod[0:64], axis=0, keepdims=True),
                                 jnp.sum(prod[64:128], axis=0, keepdims=True)], axis=1)
        dm = jnp.concatenate(halves(da, 0), axis=1)
        kk = kb[i].reshape(2 * toks, 128)
        vv = vb[i].reshape(2 * toks, 128)
        kt = kk.T
        qm = split_q(i)
        dk = dv = None
        for n in range(3):
            at = slice(n * part, (n + 1) * part)
            s = nt(kk, qm[at])
            p = jnp.exp2(s * EXP_SCALE - lse[i, :, at])
            dp = nn(vv, dm[:, at])
            ds = (p * (dp - delta[:, at])).astype(BF)
            dv_n = nt(p.astype(BF), dm[:, at])
            dk_n = nn(ds, qm[at])
            dv = dv_n if dv is None else dv + dv_n
            dk = dk_n if dk is None else dk + dk_n
            osum[:, at] = nn(kt, ds)
        dk = dk * 0.125
        dks[i, 0] = dk[toks:].astype(BF)
        dks[i, 1] = dv[toks:].astype(BF)
        give_k(i).start()
        give_v(i).start()
        dko[i, 0] = dk[:toks]
        dko[i, 1] = dv[:toks]
        both = jnp.concatenate([osum[0:64, 0:toks], osum[64:128, toks:2 * toks]], axis=0)
        gq_st[i] = (both.T * 0.125).astype(BF)
        put_q(i).start()

    def finish(i):
        give_k(i).wait_recv()
        gk_st[i] = (dko[i, 0] + dkr[i, 0].astype(F32)).astype(BF)
        put_k(i).start()
        give_v(i).wait_recv()
        gv_st[i] = (dko[i, 1] + dkr[i, 1].astype(F32)).astype(BF)
        put_v(i).start()

    def sum_up(s, sub):
        at = pl.ds(*SUBS[sub])
        return remote(rss.at[s, 0, at], rsr.at[s, 0, at], rr_s.at[s, sub], rr_r.at[s, sub], z_up)

    def sum_down(s, sub):
        at = pl.ds(*SUBS[sub])
        return remote(rss.at[s, 1, at], rsr.at[s, 1, at], rl_s.at[s, sub], rl_r.at[s, sub], z_down)

    def own_term(s):
        owner_up = lax.rem(z - 1 - s + 2 * NZ, NZ)
        owner_down = lax.rem(z + 1 + s, NZ)
        rows = jnp.concatenate([att[block_rows(owner_up, half), :],
                                att[block_rows(owner_down, half, half), :]], axis=0)
        gacc[...] = nn(rows, dcat[...])

    def sum_step(s):
        for sub, (off, size) in enumerate(SUBS):
            for way, copy in enumerate((sum_up, sum_down)):
                at = slice(way * half + off, way * half + off + size)

                @pl.when(s > 0)
                def _():
                    copy(s - 1, sub).wait_recv()
                    gacc[at, :] = gacc[at, :] + rsr[s - 1, way, off:off + size].astype(F32)

                @pl.when(s < RING)
                def _():
                    rss[s, way, off:off + size] = gacc[at, :].astype(BF)
                    copy(s, sub).start()

        @pl.when(s < RING)
        def _():
            own_term(s + 1)

    @pl.loop(0, pairs + NZ)
    def _(t):
        @pl.when(t < pairs)
        def _():
            forward(t)

        h = t - RING_AT

        @pl.when(h == 0)
        def _():
            cross_own.wait_recv()

        @pl.when((h >= 1) & (h <= RING))
        def _():
            cross(h - 1, True).wait_recv()
            cross(h - 1, False).wait_recv()

        @pl.when((h >= 0) & (h < RING))
        def _():
            ring(h)

        s = t - pairs

        @pl.when(s == 0)
        def _():
            d_swap.wait_recv()

            @pl.loop(0, pairs)
            def _(i):
                swap_att(i).wait_recv()

            own_term(0)

        @pl.when(s >= 0)
        def _():
            sum_step(s)

        @pl.when((t >= LAG) & (t < LAG + pairs))
        def _():
            backward(t - LAG)

    def sum_y(s):
        return remote(gys.at[lax.rem(y + s, NY)], gyr.at[s], gy_s.at[s], gy_r.at[s], at_y(s))

    gys[...] = nn(picker(4 * 48, blk, 48, 40, 40), gacc[...].astype(BF)).astype(BF).reshape(4, 48, cols)
    for s in range(1, NY):
        sum_y(s).start()

    @pl.loop(0, pairs - 3)
    def _(i):
        finish(i)

    summed = gys[y].astype(F32)
    for s in range(1, NY):
        sum_y(s).wait_recv()
        summed = summed + gyr[s].astype(F32)
    gxs[...] = nn(picker(64, 48, 16, 10, 10), summed.astype(BF)).astype(BF).reshape(4, 16, cols)

    def sum_x(o):
        return remote(gxs.at[o], gxr.at[x], gx_s.at[o], gx_r.at[x], dev(cam_=core, obj_=o))

    for o in range(4):
        mine = own_target & (obj == o)

        @pl.when(jnp.logical_not(mine))
        def _():
            sum_x(o).start()

        @pl.when(mine)
        def _():
            pltpu.make_async_copy(gxs.at[o], gxr.at[x], gx_r.at[x]).start()

    @pl.loop(pairs - 3, pairs)
    def _(i):
        finish(i)

    for o in range(4):
        pltpu.make_async_copy(gxs.at[o], gxr.at[o], gx_r.at[o]).wait()
    total = gxr[0].astype(F32) + gxr[1].astype(F32) + gxr[2].astype(F32) + gxr[3].astype(F32)
    gwo_ref[...] = total[0:10, :] * scale

    for t in range(4):
        @pl.when(jnp.logical_not(own_target & (x == t)))
        def _():
            w_to(t).wait_send()

        @pl.when(jnp.logical_not(own_target & (obj == t)))
        def _():
            sum_x(t).wait_send()

    for s in range(1, NY):
        y_copy(s).wait_send()
        sum_y(s).wait_send()
    d_swap.wait_send()
    cross_own.wait_send()

    @pl.loop(0, RING)
    def _(h):
        up_copy(h, 0).wait_send()
        down_copy(h, 0).wait_send()
        cross(h, True).wait_send()
        cross(h, False).wait_send()
        for sub in range(len(SUBS)):
            sum_up(h, sub).wait_send()
            sum_down(h, sub).wait_send()

    @pl.loop(0, pairs)
    def _(i):
        send_k(i).wait_send()
        send_v(i).wait_send()
        swap_att(i).wait_send()
        give_k(i).wait_send()
        give_v(i).wait_send()
        put_q(i).wait()
        put_k(i).wait()
        put_v(i).wait()


def body(queries, keys, values, d_out, w_out):
    shape = queries.shape
    width, model = queries.shape[4], d_out.shape[4]
    toks = queries.shape[1] * queries.shape[2] * queries.shape[3]
    tokens = toks * lax.axis_size("cam") * lax.axis_size("band") * lax.axis_size("obj")
    scale = float(tokens) ** -0.5
    pairs = width // 128
    cols = w_out.shape[1]
    blk = width // NZ
    dma = lambda *n: pltpu.SemaphoreType.DMA(n)
    flat = lambda a: a.reshape(toks, a.shape[4])
    any_ = pl.BlockSpec(memory_space=pl.ANY)
    vmem = pl.BlockSpec(memory_space=pltpu.VMEM)
    grad = jax.ShapeDtypeStruct((toks, width), BF)
    scratch = [
        pltpu.VMEM((pairs, toks, 128), BF),
        pltpu.VMEM((pairs, 2, toks, 128), BF),
        pltpu.VMEM((pairs, 2, toks, 128), BF),
        pltpu.VMEM((toks, model), BF),
        pltpu.VMEM((2 * toks, cols), BF),
        pltpu.VMEM((toks, cols), BF),
        pltpu.VMEM((16, cols), BF),
        pltpu.VMEM((4, 16, cols), BF),
        pltpu.VMEM((4, 48, cols), BF),
        pltpu.VMEM((width, cols), BF),
        pltpu.VMEM((width, cols), BF),
        pltpu.VMEM((width, 2 * toks), BF),
        pltpu.VMEM((pairs, 1, 2 * toks), F32),
        pltpu.VMEM((128, 2 * toks), F32),
        pltpu.VMEM((pairs, 2, toks, 128), BF),
        pltpu.VMEM((pairs, 2, toks, 128), BF),
        pltpu.VMEM((pairs, 2, toks, 128), F32),
        pltpu.VMEM((pairs, toks, 128), BF),
        pltpu.VMEM((pairs, toks, 128), BF),
        pltpu.VMEM((pairs, toks, 128), BF),
        pltpu.VMEM((blk, cols), F32),
        pltpu.VMEM((RING, 2, blk // 2, cols), BF),
        pltpu.VMEM((RING, 2, blk // 2, cols), BF),
        pltpu.VMEM((4, 48, cols), BF),
        pltpu.VMEM((4, 48, cols), BF),
        pltpu.VMEM((4, 16, cols), BF),
        pltpu.VMEM((4, 16, cols), BF),
        dma(pairs), dma(pairs), dma(pairs), pltpu.SemaphoreType.DMA,
        dma(4), dma(4), dma(4), dma(4), dma(RING), dma(RING), dma(RING), dma(RING),
        dma(2 * RING + 1), dma(2 * RING + 1), dma(pairs), dma(pairs), dma(pairs), dma(pairs),
        pltpu.SemaphoreType.DMA, pltpu.SemaphoreType.DMA, dma(pairs), dma(pairs),
        dma(pairs), dma(pairs), dma(pairs), dma(pairs),
        dma(RING, 2), dma(RING, 2), dma(RING, 2), dma(RING, 2), dma(4), dma(4), dma(4), dma(4),
        dma(pairs), dma(pairs), dma(pairs),
    ]
    gq, gk, gv, gwo = pl.pallas_call(
        functools.partial(kernel, scale),
        out_shape=(grad, grad, grad, jax.ShapeDtypeStruct(w_out.shape, F32)),
        in_specs=[any_] * 4 + [vmem],
        out_specs=(any_, any_, any_, vmem),
        scratch_shapes=scratch,
        compiler_params=pltpu.CompilerParams(
            collective_id=0, has_side_effects=True, vmem_limit_bytes=64 * 1024 * 1024 - 65536),
        name="row_attention_backward",
    )(flat(queries), flat(keys), flat(values), flat(d_out), w_out)
    return gq.reshape(shape), gk.reshape(shape), gv.reshape(shape), gwo


def solution(mesh):
    act = P("obj", "cam", "band", None, None)
    proj = P(("band", "obj"), "cam")
    return jax.shard_map(
        body,
        mesh=mesh,
        in_specs=(act, act, act, act, proj),
        out_specs=(act, act, act, proj),
        check_vma=False,
    )
```

```python
import functools
import math

import jax
import jax.numpy as jnp
from jax import lax
from jax.experimental import pallas as pl
from jax.experimental.pallas import tpu as pltpu
from jax.sharding import PartitionSpec as P

BF = jnp.bfloat16
F32 = jnp.float32
MESH = pl.DeviceIdType.MESH
NY, NZ = 4, 8
RING = NZ - 1
LAG = 6
RING_AT = 3
SUM_AT = 8
SHARED = 16
TOP, REST = pl.ds(0, 32), pl.ds(32, 16)
SUBS = ((0, 48), (48, 32))
EXP_SCALE = 0.125 / math.log(2.0)


def nn(a, b):
    return lax.dot_general(a, b, (((1,), (0,)), ((), ())), preferred_element_type=F32)


def nt(a, b):
    return lax.dot_general(a, b, (((1,), (1,)), ((), ())), preferred_element_type=F32)


def picker(rows, cols, row_step, col_step, width):
    r = lax.broadcasted_iota(jnp.int32, (rows, cols), 0)
    c = lax.broadcasted_iota(jnp.int32, (rows, cols), 1)
    pick = jnp.zeros((rows, cols), F32)
    for b in range(4):
        k = r - row_step * b
        hit = (k >= 0) & (k < width) & (c - col_step * b == k)
        pick = pick + jnp.where(hit, 1.0, 0.0).astype(F32)
    return pick.astype(BF)


def halves(x, axis):
    index = lax.broadcasted_iota(jnp.int32, x.shape, axis)
    first = jnp.where(index < x.shape[axis] // 2, x, 0.0)
    return first.astype(BF), (x - first).astype(BF)


def kernel(scale, q_hbm, k_hbm, v_hbm, d_hbm, w_ref, gq_hbm, gk_hbm, gv_hbm, gwo_ref,
           qb, kb, vb, dfull, dcat, doth, wpad, wx, wy, wown, woth, att, lse, osum,
           dks, dkr, dko, gq_st, gk_st, gv_st, gacc, rss, rsr, gys, gyr, gyf, gxs, gxr,
           q_ld, k_ld, v_ld, d_ld, wx_s, wx_r, wy_s, wy_r, zr_s, zr_r, zl_s, zl_r,
           oc_s, oc_r, wp_s, wp_r, k_s, k_r, v_s, v_r, dx_s, dx_r, at_s, at_r, dk_s, dk_r, dv_s, dv_r,
           rr_s, rr_r, rl_s, rl_r, gy_s, gy_r, gx_s, gx_r, gq_o, gk_o, gv_o):
    pairs, toks = qb.shape[0], qb.shape[1]
    cols = wpad.shape[1]
    blk = wown.shape[0] // NZ
    half = blk // 2
    cam, band, obj = lax.axis_index("cam"), lax.axis_index("band"), lax.axis_index("obj")
    z, y = band // NY, band % NY
    xh, core = obj // 2, obj % 2
    x = xh * 2 + cam
    base = (blk * z + half) // 128

    def dev(cam_=None, band_=None, obj_=None):
        return {
            "cam": cam if cam_ is None else cam_,
            "band": band if band_ is None else band_,
            "obj": obj if obj_ is None else obj_,
        }

    def at_z(shift):
        return dev(band_=lax.rem(z + shift + NZ, NZ) * NY + y)

    def at_y(shift):
        return dev(band_=z * NY + lax.rem(y + shift, NY))

    cam_peer = dev(cam_=1 - cam)
    wrap_peer = dev(cam_=1 - cam, obj_=(1 - xh) * 2 + core)
    core_peer = dev(obj_=xh * 2 + 1 - core)
    z_up, z_down = at_z(1), at_z(-1)
    y_up, y_down = at_y(1), at_y(NY - 1)

    def remote(src, dst, send, recv, device):
        return pltpu.make_async_remote_copy(
            src_ref=src, dst_ref=dst, send_sem=send, recv_sem=recv, device_id=device,
            device_id_type=MESH)

    def order(i):
        step = (i + 1) // 2
        sign = 2 * (i % 2) - 1
        return lax.rem(base + sign * step + pairs, pairs)

    def lanes(i):
        return pl.ds(pl.multiple_of(order(i) * 128, 128), 128)

    def load_q(i):
        return pltpu.make_async_copy(q_hbm.at[:, lanes(i)], qb.at[i], q_ld.at[i])

    def load_k(i):
        return pltpu.make_async_copy(k_hbm.at[:, lanes(i)], kb.at[i, 0], k_ld.at[i])

    def load_v(i):
        return pltpu.make_async_copy(v_hbm.at[:, lanes(i)], vb.at[i, 0], v_ld.at[i])

    def send_k(i):
        return remote(k_hbm.at[:, lanes(i)], kb.at[i, 1], k_s.at[i], k_r.at[i], cam_peer)

    def send_v(i):
        return remote(v_hbm.at[:, lanes(i)], vb.at[i, 1], v_s.at[i], v_r.at[i], cam_peer)

    load_d = pltpu.make_async_copy(d_hbm, dfull, d_ld)
    load_d.start()
    wpad[...] = jnp.zeros_like(wpad)
    wpad[0:10, :] = w_ref[...]

    @pl.loop(0, pairs)
    def _(i):
        load_q(i).start()
        load_k(i).start()
        load_v(i).start()

    barrier = pltpu.get_barrier_semaphore()
    peers = [dev(cam_=lax.rem(cam + a, 2), obj_=lax.rem(obj + b, 4))
             for a in range(2) for b in range(4) if a + b > 0]
    peers += [y_up, y_down, z_up, z_down]
    for peer in peers:
        pl.semaphore_signal(barrier, inc=1, device_id=peer, device_id_type=MESH)
    pl.semaphore_wait(barrier, len(peers))

    def w_to(t):
        return remote(wpad, wx.at[obj], wx_s.at[t], wx_r.at[obj],
                      dev(cam_=t % 2, obj_=(t // 2) * 2 + cam))

    own_target = core == cam
    for t in range(4):
        mine = own_target & (x == t)

        @pl.when(jnp.logical_not(mine))
        def _():
            w_to(t).start()

    @pl.when(own_target)
    def _():
        pltpu.make_async_copy(wpad, wx.at[obj], wx_r.at[obj]).start()

    @pl.loop(0, pairs)
    def _(i):
        send_k(i).start()
        send_v(i).start()

    join_x = picker(48, 64, 10, 16, 10)
    for o in range(4):
        pltpu.make_async_copy(wpad, wx.at[o], wx_r.at[o]).wait()
    joined = nn(join_x, wx[...].reshape(64, cols)).astype(BF)
    wy[y] = joined

    def y_copy(n):
        block = (y, y, y, y, lax.rem(y + NY - 1, NY), lax.rem(y + 1, NY))[n]
        rows = (TOP, REST, REST, TOP, TOP, REST)[n]
        return remote(wy.at[block, rows], wy.at[block, rows], wy_s.at[n], wy_r.at[n],
                      y_down if n % 2 else y_up)

    for n in range(4):
        y_copy(n).start()

    load_d.wait()
    low, high = dfull[:, 0:cols], dfull[:, cols:2 * cols]

    @pl.when(core == 0)
    def _():
        dcat[0:toks, :] = low
        doth[...] = high

    @pl.when(core == 1)
    def _():
        dcat[0:toks, :] = high
        doth[...] = low

    d_swap = remote(doth, dcat.at[pl.ds(toks, toks)], dx_s, dx_r, core_peer)
    d_swap.start()

    join_y = picker(blk, 4 * 48, 40, 48, 40)
    for n in range(2):
        y_copy(n).wait_recv()
        y_copy(n + 4).start()
    for n in range(2, 6):
        y_copy(n).wait_recv()

    def block_rows(b, size=None, off=0):
        return pl.ds(pl.multiple_of(b * blk + off, 16), blk if size is None else size)

    wown[block_rows(z), :] = nn(join_y, wy[...].reshape(4 * 48, cols)).astype(BF)

    def up_copy(h, back):
        b = lax.rem(z - h // 2 - back + NZ, NZ)
        rows = block_rows(b, half - SHARED, (h % 2) * half + SHARED * xh)
        return remote(wown.at[rows], wown.at[rows], zr_s.at[h], zr_r.at[h], z_up)

    def down_copy(h, back):
        b = lax.rem(z + h // 2 + back, NZ)
        rows = block_rows(b, half - SHARED, (1 - h % 2) * half + SHARED * xh)
        return remote(wown.at[rows], wown.at[rows], zl_s.at[h], zl_r.at[h], z_down)

    def cross(h, up, kind=None):
        b = lax.rem(z - h // 2 - 1 + NZ, NZ) if up else lax.rem(z + h // 2 + 1, NZ)
        j = h % 2 if up else 1 - h % 2
        n = 2 * h + (0 if up else 1)
        if kind is not None:
            rows = block_rows(b, SHARED, j * half + (half - SHARED) * kind)
            return remote(wown.at[rows], wown.at[rows], wp_s.at[n], wp_r.at[n], wrap_peer)
        rows = block_rows(b, half, j * half)
        return remote(wown.at[rows], woth.at[rows], oc_s.at[n], oc_r.at[n], core_peer)

    own_rows = block_rows(z)
    cross_own = remote(wown.at[own_rows], woth.at[own_rows], oc_s.at[2 * RING], oc_r.at[2 * RING], core_peer)
    for h in range(2):
        up_copy(h, 0).start()
        down_copy(h, 0).start()
    cross_own.start()

    def ring(h):
        up_copy(h, 1).wait_recv()

        @pl.when(h + 2 < RING)
        def _():
            up_copy(h + 2, 0).start()

        down_copy(h, 1).wait_recv()

        @pl.when(h + 2 < RING)
        def _():
            down_copy(h + 2, 0).start()

        cross(h, True, xh).start()
        cross(h, False, xh).start()

    def split_q(i):
        first, second = halves(qb[i].astype(F32), 1)
        return jnp.concatenate([first, second], axis=0)

    def swap_att(i):
        rows = pl.ds(pl.multiple_of(order(i) * 128, 128), 128)
        return remote(att.at[rows, pl.ds(0, toks)], att.at[rows, pl.ds(toks, toks)],
                      at_s.at[i], at_r.at[i], core_peer)

    part = 2 * toks // 3

    def forward(i):
        load_q(i).wait()
        load_k(i).wait()
        load_v(i).wait()
        send_k(i).wait_recv()
        send_v(i).wait_recv()
        kk = kb[i].reshape(2 * toks, 128)
        vt = vb[i].reshape(2 * toks, 128).T
        qm = split_q(i)
        for n in range(3):
            s = nt(kk, qm[n * part:(n + 1) * part])
            top = jnp.max(s, axis=0, keepdims=True)
            e = jnp.exp2((s - top) * EXP_SCALE)
            total = jnp.sum(e, axis=0, keepdims=True)
            osum[:, n * part:(n + 1) * part] = nn(vt, e.astype(BF)) * (1.0 / total)
            lse[i, :, n * part:(n + 1) * part] = top * EXP_SCALE + jnp.log2(total)
        rows = pl.ds(pl.multiple_of(order(i) * 128, 128), 128)
        both = jnp.concatenate([osum[0:64, 0:toks], osum[64:128, toks:2 * toks]], axis=0)
        att[rows, 0:toks] = both.astype(BF)
        swap_att(i).start()

    def give_k(i):
        return remote(dks.at[i, 0], dkr.at[i, 0], dk_s.at[i], dk_r.at[i], cam_peer)

    def give_v(i):
        return remote(dks.at[i, 1], dkr.at[i, 1], dv_s.at[i], dv_r.at[i], cam_peer)

    def put_q(i):
        return pltpu.make_async_copy(gq_st.at[i], gq_hbm.at[:, lanes(i)], gq_o.at[i])

    def put_k(i):
        return pltpu.make_async_copy(gk_st.at[i], gk_hbm.at[:, lanes(i)], gk_o.at[i])

    def put_v(i):
        return pltpu.make_async_copy(gv_st.at[i], gv_hbm.at[:, lanes(i)], gv_o.at[i])

    def backward(i):
        rows = pl.ds(pl.multiple_of(order(i) * 128, 128), 128)
        da = nt(wown[rows, :], dcat[0:toks, :]) + nt(woth[rows, :], doth[...])
        da = da.astype(BF).astype(F32)
        prod = da * att[rows, 0:toks].astype(F32)
        delta = jnp.concatenate([jnp.sum(prod[0:64], axis=0, keepdims=True),
                                 jnp.sum(prod[64:128], axis=0, keepdims=True)], axis=1)
        dm = jnp.concatenate(halves(da, 0), axis=1)
        kk = kb[i].reshape(2 * toks, 128)
        vv = vb[i].reshape(2 * toks, 128)
        kt = kk.T
        qm = split_q(i)
        dk = dv = None
        for n in range(3):
            at = slice(n * part, (n + 1) * part)
            s = nt(kk, qm[at])
            p = jnp.exp2(s * EXP_SCALE - lse[i, :, at])
            dp = nn(vv, dm[:, at])
            ds = (p * (dp - delta[:, at])).astype(BF)
            dv_n = nt(p.astype(BF), dm[:, at])
            dk_n = nn(ds, qm[at])
            dv = dv_n if dv is None else dv + dv_n
            dk = dk_n if dk is None else dk + dk_n
            osum[:, at] = nn(kt, ds)
        dk = dk * 0.125
        dks[i, 0] = dk[toks:].astype(BF)
        dks[i, 1] = dv[toks:].astype(BF)
        give_k(i).start()
        give_v(i).start()
        dko[i, 0] = dk[:toks]
        dko[i, 1] = dv[:toks]
        both = jnp.concatenate([osum[0:64, 0:toks], osum[64:128, toks:2 * toks]], axis=0)
        gq_st[i] = (both.T * 0.125).astype(BF)
        put_q(i).start()

    def finish(i):
        give_k(i).wait_recv()
        gk_st[i] = (dko[i, 0] + dkr[i, 0].astype(F32)).astype(BF)
        put_k(i).start()
        give_v(i).wait_recv()
        gv_st[i] = (dko[i, 1] + dkr[i, 1].astype(F32)).astype(BF)
        put_v(i).start()

    def sum_up(s, sub):
        at = pl.ds(*SUBS[sub])
        return remote(rss.at[s, 0, at], rsr.at[s, 0, at], rr_s.at[s, sub], rr_r.at[s, sub], z_up)

    def sum_down(s, sub):
        at = pl.ds(*SUBS[sub])
        return remote(rss.at[s, 1, at], rsr.at[s, 1, at], rl_s.at[s, sub], rl_r.at[s, sub], z_down)

    def own_term(s):
        owner_up = lax.rem(z - 1 - s + 2 * NZ, NZ)
        owner_down = lax.rem(z + 1 + s, NZ)
        rows = jnp.concatenate([att[block_rows(owner_up, half), :],
                                att[block_rows(owner_down, half, half), :]], axis=0)
        gacc[...] = nn(rows, dcat[...])

    def sum_step(s):
        for sub, (off, size) in enumerate(SUBS):
            for way, copy in enumerate((sum_up, sum_down)):
                at = slice(way * half + off, way * half + off + size)

                @pl.when(s > 0)
                def _():
                    copy(s - 1, sub).wait_recv()
                    gacc[at, :] = gacc[at, :] + rsr[s - 1, way, off:off + size].astype(F32)

                @pl.when(s < RING)
                def _():
                    rss[s, way, off:off + size] = gacc[at, :].astype(BF)
                    copy(s, sub).start()

        @pl.when(s < RING)
        def _():
            own_term(s + 1)

    @pl.loop(0, max(LAG + pairs, SUM_AT + NZ))
    def _(t):
        @pl.when(t < pairs)
        def _():
            forward(t)

        h = t - RING_AT

        @pl.when(h == 0)
        def _():
            cross_own.wait_recv()

        @pl.when((h >= 2) & (h <= RING + 1))
        def _():
            cross(h - 2, True).wait_recv()
            cross(h - 2, False).wait_recv()

        @pl.when((h >= 1) & (h <= RING))
        def _():
            for up in (True, False):
                cross(h - 1, up, 1 - xh).wait_recv()
                cross(h - 1, up).start()

        @pl.when((h >= 0) & (h < RING))
        def _():
            ring(h)

        @pl.when((t >= 1) & (t < pairs))
        def _():
            swap_att(t - 1).wait_recv()

        @pl.when(t == pairs - 1)
        def _():
            swap_att(t).wait_recv()

        s = t - SUM_AT

        @pl.when(s == 0)
        def _():
            d_swap.wait_recv()
            own_term(0)

        @pl.when((s >= 0) & (s < NZ))
        def _():
            sum_step(s)

        @pl.when((t >= LAG) & (t < LAG + pairs))
        def _():
            backward(t - LAG)

    y_next, y_last = lax.rem(y + 1, NY), lax.rem(y + NY - 1, NY)
    y_far = lax.rem(y + 2, NY)

    def sum_y(n):
        rows = (TOP, REST, REST, TOP, TOP, REST)[n]
        src = (gys.at[y_far], gys.at[y_far], gys.at[y_next], gys.at[y_last], gyf, gyf)[n]
        dst = (0, 1, 2, 3, 2, 3)[n]
        return remote(src.at[rows], gyr.at[dst, rows], gy_s.at[n], gy_r.at[n],
                      y_down if n % 2 else y_up)

    gys[...] = nn(picker(4 * 48, blk, 48, 40, 40), gacc[...].astype(BF)).astype(BF).reshape(4, 48, cols)
    for n in range(4):
        sum_y(n).start()

    @pl.loop(0, pairs - 6)
    def _(i):
        finish(i)

    sum_y(0).wait_recv()
    gyf[0:32] = (gys[y_next, 0:32].astype(F32) + gyr[0, 0:32].astype(F32)).astype(BF)
    sum_y(4).start()
    sum_y(1).wait_recv()
    gyf[32:48] = (gys[y_last, 32:48].astype(F32) + gyr[1, 32:48].astype(F32)).astype(BF)
    sum_y(5).start()

    @pl.loop(pairs - 6, pairs - 3)
    def _(i):
        finish(i)

    for n in range(2, 6):
        sum_y(n).wait_recv()
    summed = gys[y].astype(F32) + gyr[2].astype(F32) + gyr[3].astype(F32)
    gxs[...] = nn(picker(64, 48, 16, 10, 10), summed.astype(BF)).astype(BF).reshape(4, 16, cols)

    def sum_x(o):
        return remote(gxs.at[o], gxr.at[x], gx_s.at[o], gx_r.at[x], dev(cam_=core, obj_=o))

    for o in range(4):
        mine = own_target & (obj == o)

        @pl.when(jnp.logical_not(mine))
        def _():
            sum_x(o).start()

        @pl.when(mine)
        def _():
            pltpu.make_async_copy(gxs.at[o], gxr.at[x], gx_r.at[x]).start()

    @pl.loop(pairs - 3, pairs)
    def _(i):
        finish(i)

    for o in range(4):
        pltpu.make_async_copy(gxs.at[o], gxr.at[o], gx_r.at[o]).wait()
    total = gxr[0].astype(F32) + gxr[1].astype(F32) + gxr[2].astype(F32) + gxr[3].astype(F32)
    gwo_ref[...] = total[0:10, :] * scale

    for t in range(4):
        @pl.when(jnp.logical_not(own_target & (x == t)))
        def _():
            w_to(t).wait_send()

        @pl.when(jnp.logical_not(own_target & (obj == t)))
        def _():
            sum_x(t).wait_send()

    for n in range(6):
        y_copy(n).wait_send()
        sum_y(n).wait_send()
    d_swap.wait_send()
    cross_own.wait_send()

    @pl.loop(0, RING)
    def _(h):
        up_copy(h, 0).wait_send()
        down_copy(h, 0).wait_send()
        for up in (True, False):
            cross(h, up).wait_send()
            cross(h, up, xh).wait_send()
        for sub in range(len(SUBS)):
            sum_up(h, sub).wait_send()
            sum_down(h, sub).wait_send()

    @pl.loop(0, pairs)
    def _(i):
        send_k(i).wait_send()
        send_v(i).wait_send()
        swap_att(i).wait_send()
        give_k(i).wait_send()
        give_v(i).wait_send()
        put_q(i).wait()
        put_k(i).wait()
        put_v(i).wait()


def body(queries, keys, values, d_out, w_out):
    shape = queries.shape
    width, model = queries.shape[4], d_out.shape[4]
    toks = queries.shape[1] * queries.shape[2] * queries.shape[3]
    tokens = toks * lax.axis_size("cam") * lax.axis_size("band") * lax.axis_size("obj")
    scale = float(tokens) ** -0.5
    pairs = width // 128
    cols = w_out.shape[1]
    blk = width // NZ
    dma = lambda *n: pltpu.SemaphoreType.DMA(n)
    flat = lambda a: a.reshape(toks, a.shape[4])
    any_ = pl.BlockSpec(memory_space=pl.ANY)
    vmem = pl.BlockSpec(memory_space=pltpu.VMEM)
    grad = jax.ShapeDtypeStruct((toks, width), BF)
    scratch = [
        pltpu.VMEM((pairs, toks, 128), BF),
        pltpu.VMEM((pairs, 2, toks, 128), BF),
        pltpu.VMEM((pairs, 2, toks, 128), BF),
        pltpu.VMEM((toks, model), BF),
        pltpu.VMEM((2 * toks, cols), BF),
        pltpu.VMEM((toks, cols), BF),
        pltpu.VMEM((16, cols), BF),
        pltpu.VMEM((4, 16, cols), BF),
        pltpu.VMEM((4, 48, cols), BF),
        pltpu.VMEM((width, cols), BF),
        pltpu.VMEM((width, cols), BF),
        pltpu.VMEM((width, 2 * toks), BF),
        pltpu.VMEM((pairs, 1, 2 * toks), F32),
        pltpu.VMEM((128, 2 * toks), F32),
        pltpu.VMEM((pairs, 2, toks, 128), BF),
        pltpu.VMEM((pairs, 2, toks, 128), BF),
        pltpu.VMEM((pairs, 2, toks, 128), F32),
        pltpu.VMEM((pairs, toks, 128), BF),
        pltpu.VMEM((pairs, toks, 128), BF),
        pltpu.VMEM((pairs, toks, 128), BF),
        pltpu.VMEM((blk, cols), F32),
        pltpu.VMEM((RING, 2, blk // 2, cols), BF),
        pltpu.VMEM((RING, 2, blk // 2, cols), BF),
        pltpu.VMEM((4, 48, cols), BF),
        pltpu.VMEM((4, 48, cols), BF),
        pltpu.VMEM((48, cols), BF),
        pltpu.VMEM((4, 16, cols), BF),
        pltpu.VMEM((4, 16, cols), BF),
        dma(pairs), dma(pairs), dma(pairs), pltpu.SemaphoreType.DMA,
        dma(4), dma(4), dma(6), dma(6), dma(RING), dma(RING), dma(RING), dma(RING),
        dma(2 * RING + 1), dma(2 * RING + 1), dma(2 * RING), dma(2 * RING), dma(pairs), dma(pairs), dma(pairs), dma(pairs),
        pltpu.SemaphoreType.DMA, pltpu.SemaphoreType.DMA, dma(pairs), dma(pairs),
        dma(pairs), dma(pairs), dma(pairs), dma(pairs),
        dma(RING, 2), dma(RING, 2), dma(RING, 2), dma(RING, 2), dma(6), dma(6), dma(4), dma(4),
        dma(pairs), dma(pairs), dma(pairs),
    ]
    gq, gk, gv, gwo = pl.pallas_call(
        functools.partial(kernel, scale),
        out_shape=(grad, grad, grad, jax.ShapeDtypeStruct(w_out.shape, F32)),
        in_specs=[any_] * 4 + [vmem],
        out_specs=(any_, any_, any_, vmem),
        scratch_shapes=scratch,
        compiler_params=pltpu.CompilerParams(
            collective_id=0, has_side_effects=True, vmem_limit_bytes=64 * 1024 * 1024 - 65536),
        name="row_attention_backward",
    )(flat(queries), flat(keys), flat(values), flat(d_out), w_out)
    return gq.reshape(shape), gk.reshape(shape), gv.reshape(shape), gwo


def solution(mesh):
    act = P("obj", "cam", "band", None, None)
    proj = P(("band", "obj"), "cam")
    return jax.shard_map(
        body,
        mesh=mesh,
        in_specs=(act, act, act, act, proj),
        out_specs=(act, act, act, proj),
        check_vma=False,
    )
```

```python
import functools
import math

import jax
import jax.numpy as jnp
from jax import lax
from jax.experimental import pallas as pl
from jax.experimental.pallas import tpu as pltpu
from jax.sharding import PartitionSpec as P

BF = jnp.bfloat16
F32 = jnp.float32
MESH = pl.DeviceIdType.MESH
NY, NZ = 4, 8
RING = NZ - 1
LAG = 6
RING_AT = 3
SUM_AT = 8
SHARED = 16
TOP, REST = pl.ds(0, 32), pl.ds(32, 16)
SUBS = ((0, 48), (48, 32))
EXP_SCALE = 0.125 / math.log(2.0)


def nn(a, b):
    return lax.dot_general(a, b, (((1,), (0,)), ((), ())), preferred_element_type=F32)


def nt(a, b):
    return lax.dot_general(a, b, (((1,), (1,)), ((), ())), preferred_element_type=F32)


def picker(rows, cols, row_step, col_step, width):
    r = lax.broadcasted_iota(jnp.int32, (rows, cols), 0)
    c = lax.broadcasted_iota(jnp.int32, (rows, cols), 1)
    pick = jnp.zeros((rows, cols), F32)
    for b in range(4):
        k = r - row_step * b
        hit = (k >= 0) & (k < width) & (c - col_step * b == k)
        pick = pick + jnp.where(hit, 1.0, 0.0).astype(F32)
    return pick.astype(BF)


def halves(x, axis):
    index = lax.broadcasted_iota(jnp.int32, x.shape, axis)
    first = jnp.where(index < x.shape[axis] // 2, x, 0.0)
    return first.astype(BF), (x - first).astype(BF)


def kernel(scale, q_hbm, k_hbm, v_hbm, d_hbm, w_ref, gq_hbm, gk_hbm, gv_hbm, gwo_ref,
           qb, kb, vb, dfull, dcat, doth, wpad, wx, wy, wown, woth, att, lse, osum,
           dks, dkr, dko, gq_st, gk_st, gv_st, gacc, rss, rsr, gys, gyr, gyf, gxs, gxr,
           q_ld, k_ld, v_ld, d_ld, wx_s, wx_r, wy_s, wy_r, zr_s, zr_r, zl_s, zl_r,
           oc_s, oc_r, wp_s, wp_r, k_s, k_r, v_s, v_r, dx_s, dx_r, at_s, at_r, dk_s, dk_r, dv_s, dv_r,
           rr_s, rr_r, rl_s, rl_r, gy_s, gy_r, gx_s, gx_r, gq_o, gk_o, gv_o):
    pairs, toks = qb.shape[0], qb.shape[1]
    cols = wpad.shape[1]
    blk = wown.shape[0] // NZ
    half = blk // 2
    cam, band, obj = lax.axis_index("cam"), lax.axis_index("band"), lax.axis_index("obj")
    z, y = band // NY, band % NY
    xh, core = obj // 2, obj % 2
    x = xh * 2 + cam
    base = (blk * z + half) // 128

    def dev(cam_=None, band_=None, obj_=None):
        return {
            "cam": cam if cam_ is None else cam_,
            "band": band if band_ is None else band_,
            "obj": obj if obj_ is None else obj_,
        }

    def at_z(shift):
        return dev(band_=lax.rem(z + shift + NZ, NZ) * NY + y)

    def at_y(shift):
        return dev(band_=z * NY + lax.rem(y + shift, NY))

    cam_peer = dev(cam_=1 - cam)
    wrap_peer = dev(cam_=1 - cam, obj_=(1 - xh) * 2 + core)
    core_peer = dev(obj_=xh * 2 + 1 - core)
    z_up, z_down = at_z(1), at_z(-1)
    y_up, y_down = at_y(1), at_y(NY - 1)

    def remote(src, dst, send, recv, device):
        return pltpu.make_async_remote_copy(
            src_ref=src, dst_ref=dst, send_sem=send, recv_sem=recv, device_id=device,
            device_id_type=MESH)

    def order(i):
        step = (i + 1) // 2
        sign = 2 * (i % 2) - 1
        return lax.rem(base + sign * step + pairs, pairs)

    def lanes(i):
        return pl.ds(pl.multiple_of(order(i) * 128, 128), 128)

    def load_q(i):
        return pltpu.make_async_copy(q_hbm.at[:, lanes(i)], qb.at[i], q_ld.at[i])

    def load_k(i):
        return pltpu.make_async_copy(k_hbm.at[:, lanes(i)], kb.at[i, 0], k_ld.at[i])

    def load_v(i):
        return pltpu.make_async_copy(v_hbm.at[:, lanes(i)], vb.at[i, 0], v_ld.at[i])

    def send_k(i):
        return remote(k_hbm.at[:, lanes(i)], kb.at[i, 1], k_s.at[i], k_r.at[i], cam_peer)

    def send_v(i):
        return remote(v_hbm.at[:, lanes(i)], vb.at[i, 1], v_s.at[i], v_r.at[i], cam_peer)

    load_d = pltpu.make_async_copy(d_hbm, dfull, d_ld)
    load_d.start()
    wpad[...] = jnp.zeros_like(wpad)
    wpad[0:10, :] = w_ref[...]

    @pl.loop(0, pairs)
    def _(i):
        load_q(i).start()
        load_k(i).start()
        load_v(i).start()

    barrier = pltpu.get_barrier_semaphore()
    peers = [dev(cam_=lax.rem(cam + a, 2), obj_=lax.rem(obj + b, 4))
             for a in range(2) for b in range(4) if a + b > 0]
    peers += [y_up, y_down, z_up, z_down]
    for peer in peers:
        pl.semaphore_signal(barrier, inc=1, device_id=peer, device_id_type=MESH)
    pl.semaphore_wait(barrier, len(peers))

    def w_to(t):
        return remote(wpad, wx.at[obj], wx_s.at[t], wx_r.at[obj],
                      dev(cam_=t % 2, obj_=(t // 2) * 2 + cam))

    own_target = core == cam
    for t in range(4):
        mine = own_target & (x == t)

        @pl.when(jnp.logical_not(mine))
        def _():
            w_to(t).start()

    @pl.when(own_target)
    def _():
        pltpu.make_async_copy(wpad, wx.at[obj], wx_r.at[obj]).start()

    @pl.loop(0, pairs)
    def _(i):
        send_k(i).start()
        send_v(i).start()

    join_x = picker(48, 64, 10, 16, 10)
    for o in range(4):
        pltpu.make_async_copy(wpad, wx.at[o], wx_r.at[o]).wait()
    joined = nn(join_x, wx[...].reshape(64, cols)).astype(BF)
    wy[y] = joined

    def y_copy(n):
        block = (y, y, y, y, lax.rem(y + NY - 1, NY), lax.rem(y + 1, NY))[n]
        rows = (TOP, REST, REST, TOP, TOP, REST)[n]
        return remote(wy.at[block, rows], wy.at[block, rows], wy_s.at[n], wy_r.at[n],
                      y_down if n % 2 else y_up)

    for n in range(4):
        y_copy(n).start()

    load_d.wait()
    low, high = dfull[:, 0:cols], dfull[:, cols:2 * cols]

    @pl.when(core == 0)
    def _():
        dcat[0:toks, :] = low
        doth[...] = high

    @pl.when(core == 1)
    def _():
        dcat[0:toks, :] = high
        doth[...] = low

    d_swap = remote(doth, dcat.at[pl.ds(toks, toks)], dx_s, dx_r, core_peer)
    d_swap.start()

    join_y = picker(blk, 4 * 48, 40, 48, 40)
    for n in range(2):
        y_copy(n).wait_recv()
        y_copy(n + 4).start()
    for n in range(2, 6):
        y_copy(n).wait_recv()

    def block_rows(b, size=None, off=0):
        return pl.ds(pl.multiple_of(b * blk + off, 16), blk if size is None else size)

    wown[block_rows(z), :] = nn(join_y, wy[...].reshape(4 * 48, cols)).astype(BF)

    def up_copy(h, back):
        b = lax.rem(z - h // 2 - back + NZ, NZ)
        rows = block_rows(b, half - SHARED, (h % 2) * half + SHARED * xh)
        return remote(wown.at[rows], wown.at[rows], zr_s.at[h], zr_r.at[h], z_up)

    def down_copy(h, back):
        b = lax.rem(z + h // 2 + back, NZ)
        rows = block_rows(b, half - SHARED, (1 - h % 2) * half + SHARED * xh)
        return remote(wown.at[rows], wown.at[rows], zl_s.at[h], zl_r.at[h], z_down)

    def cross(h, up, kind=None):
        b = lax.rem(z - h // 2 - 1 + NZ, NZ) if up else lax.rem(z + h // 2 + 1, NZ)
        j = h % 2 if up else 1 - h % 2
        n = 2 * h + (0 if up else 1)
        if kind is not None:
            rows = block_rows(b, SHARED, j * half + (half - SHARED) * kind)
            return remote(wown.at[rows], wown.at[rows], wp_s.at[n], wp_r.at[n], wrap_peer)
        rows = block_rows(b, half, j * half)
        return remote(wown.at[rows], woth.at[rows], oc_s.at[n], oc_r.at[n], core_peer)

    own_rows = block_rows(z)
    cross_own = remote(wown.at[own_rows], woth.at[own_rows], oc_s.at[2 * RING], oc_r.at[2 * RING], core_peer)
    for h in range(2):
        up_copy(h, 0).start()
        down_copy(h, 0).start()
    cross_own.start()

    def ring(h):
        up_copy(h, 1).wait_recv()

        @pl.when(h + 2 < RING)
        def _():
            up_copy(h + 2, 0).start()

        down_copy(h, 1).wait_recv()

        @pl.when(h + 2 < RING)
        def _():
            down_copy(h + 2, 0).start()

        cross(h, True, xh).start()
        cross(h, False, xh).start()

    def split_q(i):
        first, second = halves(qb[i].astype(F32), 1)
        return jnp.concatenate([first, second], axis=0)

    def swap_att(i):
        rows = pl.ds(pl.multiple_of(order(i) * 128, 128), 128)
        return remote(att.at[rows, pl.ds(0, toks)], att.at[rows, pl.ds(toks, toks)],
                      at_s.at[i], at_r.at[i], core_peer)

    part = 2 * toks // 3

    def forward(i):
        load_q(i).wait()
        load_k(i).wait()
        load_v(i).wait()
        send_k(i).wait_recv()
        send_v(i).wait_recv()
        kk = kb[i].reshape(2 * toks, 128)
        vt = vb[i].reshape(2 * toks, 128).T
        qm = split_q(i)
        for n in range(3):
            s = nt(kk, qm[n * part:(n + 1) * part])
            top = jnp.max(s, axis=0, keepdims=True)
            e = jnp.exp2((s - top) * EXP_SCALE)
            total = jnp.sum(e, axis=0, keepdims=True)
            osum[:, n * part:(n + 1) * part] = nn(vt, e.astype(BF)) * (1.0 / total)
            lse[i, :, n * part:(n + 1) * part] = top * EXP_SCALE + jnp.log2(total)
        rows = pl.ds(pl.multiple_of(order(i) * 128, 128), 128)
        both = jnp.concatenate([osum[0:64, 0:toks], osum[64:128, toks:2 * toks]], axis=0)
        att[rows, 0:toks] = both.astype(BF)
        swap_att(i).start()

    def give_k(i):
        return remote(dks.at[i, 0], dkr.at[i, 0], dk_s.at[i], dk_r.at[i], cam_peer)

    def give_v(i):
        return remote(dks.at[i, 1], dkr.at[i, 1], dv_s.at[i], dv_r.at[i], cam_peer)

    def put_q(i):
        return pltpu.make_async_copy(gq_st.at[i], gq_hbm.at[:, lanes(i)], gq_o.at[i])

    def put_k(i):
        return pltpu.make_async_copy(gk_st.at[i], gk_hbm.at[:, lanes(i)], gk_o.at[i])

    def put_v(i):
        return pltpu.make_async_copy(gv_st.at[i], gv_hbm.at[:, lanes(i)], gv_o.at[i])

    def backward(i):
        rows = pl.ds(pl.multiple_of(order(i) * 128, 128), 128)
        da = nt(wown[rows, :], dcat[0:toks, :]) + nt(woth[rows, :], doth[...])
        da = da.astype(BF).astype(F32)
        prod = da * att[rows, 0:toks].astype(F32)
        delta = jnp.concatenate([jnp.sum(prod[0:64], axis=0, keepdims=True),
                                 jnp.sum(prod[64:128], axis=0, keepdims=True)], axis=1)
        dm = jnp.concatenate(halves(da, 0), axis=1)
        kk = kb[i].reshape(2 * toks, 128)
        vv = vb[i].reshape(2 * toks, 128)
        kt = kk.T
        qm = split_q(i)
        dk = dv = None
        for n in range(3):
            at = slice(n * part, (n + 1) * part)
            s = nt(kk, qm[at])
            p = jnp.exp2(s * EXP_SCALE - lse[i, :, at])
            dp = nn(vv, dm[:, at])
            ds = (p * (dp - delta[:, at])).astype(BF)
            dv_n = nt(p.astype(BF), dm[:, at])
            dk_n = nn(ds, qm[at])
            dv = dv_n if dv is None else dv + dv_n
            dk = dk_n if dk is None else dk + dk_n
            osum[:, at] = nn(kt, ds)
        dk = dk * 0.125
        dks[i, 0] = dk[toks:].astype(BF)
        dks[i, 1] = dv[toks:].astype(BF)
        give_k(i).start()
        give_v(i).start()
        dko[i, 0] = dk[:toks]
        dko[i, 1] = dv[:toks]
        both = jnp.concatenate([osum[0:64, 0:toks], osum[64:128, toks:2 * toks]], axis=0)
        gq_st[i] = (both.T * 0.125).astype(BF)
        put_q(i).start()

    def finish(i):
        give_k(i).wait_recv()
        gk_st[i] = (dko[i, 0] + dkr[i, 0].astype(F32)).astype(BF)
        put_k(i).start()
        give_v(i).wait_recv()
        gv_st[i] = (dko[i, 1] + dkr[i, 1].astype(F32)).astype(BF)
        put_v(i).start()

    def sum_up(s, sub):
        at = pl.ds(*SUBS[sub])
        return remote(rss.at[s, 0, at], rsr.at[s, 0, at], rr_s.at[s, sub], rr_r.at[s, sub], z_up)

    def sum_down(s, sub):
        at = pl.ds(*SUBS[sub])
        return remote(rss.at[s, 1, at], rsr.at[s, 1, at], rl_s.at[s, sub], rl_r.at[s, sub], z_down)

    def own_term(s):
        owner_up = lax.rem(z - 1 - s + 2 * NZ, NZ)
        owner_down = lax.rem(z + 1 + s, NZ)
        rows = jnp.concatenate([att[block_rows(owner_up, half), :],
                                att[block_rows(owner_down, half, half), :]], axis=0)
        gacc[...] = nn(rows, dcat[...])

    def sum_step(s, sub):
        off, size = SUBS[sub]
        for way, copy in enumerate((sum_up, sum_down)):
            at = slice(way * half + off, way * half + off + size)

            @pl.when(s > 0)
            def _():
                copy(s - 1, sub).wait_recv()
                gacc[at, :] = gacc[at, :] + rsr[s - 1, way, off:off + size].astype(F32)

            @pl.when(s < RING)
            def _():
                rss[s, way, off:off + size] = gacc[at, :].astype(BF)
                copy(s, sub).start()

    @pl.loop(0, max(LAG + pairs, SUM_AT + NZ))
    def _(t):
        @pl.when(t < pairs)
        def _():
            forward(t)

        h = t - RING_AT

        @pl.when(h == 0)
        def _():
            cross_own.wait_recv()

        @pl.when((h >= 2) & (h <= RING + 1))
        def _():
            cross(h - 2, True).wait_recv()
            cross(h - 2, False).wait_recv()

        @pl.when((h >= 1) & (h <= RING))
        def _():
            for up in (True, False):
                cross(h - 1, up, 1 - xh).wait_recv()
                cross(h - 1, up).start()

        @pl.when((h >= 0) & (h < RING))
        def _():
            ring(h)

        @pl.when((t >= 1) & (t < pairs))
        def _():
            swap_att(t - 1).wait_recv()

        @pl.when(t == pairs - 1)
        def _():
            swap_att(t).wait_recv()

        s = t - SUM_AT

        @pl.when(s == 0)
        def _():
            d_swap.wait_recv()
            own_term(0)

        @pl.when((s >= 0) & (s < NZ))
        def _():
            sum_step(s, 0)

        @pl.when((t >= LAG) & (t < LAG + pairs))
        def _():
            backward(t - LAG)

        @pl.when((s >= 0) & (s < NZ))
        def _():
            sum_step(s, 1)

        @pl.when((s >= 0) & (s < RING))
        def _():
            own_term(s + 1)

    y_next, y_last = lax.rem(y + 1, NY), lax.rem(y + NY - 1, NY)
    y_far = lax.rem(y + 2, NY)

    def sum_y(n):
        rows = (TOP, REST, REST, TOP, TOP, REST)[n]
        src = (gys.at[y_far], gys.at[y_far], gys.at[y_next], gys.at[y_last], gyf, gyf)[n]
        dst = (0, 1, 2, 3, 2, 3)[n]
        return remote(src.at[rows], gyr.at[dst, rows], gy_s.at[n], gy_r.at[n],
                      y_down if n % 2 else y_up)

    gys[...] = nn(picker(4 * 48, blk, 48, 40, 40), gacc[...].astype(BF)).astype(BF).reshape(4, 48, cols)
    for n in range(4):
        sum_y(n).start()

    @pl.loop(0, pairs - 6)
    def _(i):
        finish(i)

    sum_y(0).wait_recv()
    gyf[0:32] = (gys[y_next, 0:32].astype(F32) + gyr[0, 0:32].astype(F32)).astype(BF)
    sum_y(4).start()
    sum_y(1).wait_recv()
    gyf[32:48] = (gys[y_last, 32:48].astype(F32) + gyr[1, 32:48].astype(F32)).astype(BF)
    sum_y(5).start()

    @pl.loop(pairs - 6, pairs - 3)
    def _(i):
        finish(i)

    for n in range(2, 6):
        sum_y(n).wait_recv()
    summed = gys[y].astype(F32) + gyr[2].astype(F32) + gyr[3].astype(F32)
    gxs[...] = nn(picker(64, 48, 16, 10, 10), summed.astype(BF)).astype(BF).reshape(4, 16, cols)

    def sum_x(o):
        return remote(gxs.at[o], gxr.at[x], gx_s.at[o], gx_r.at[x], dev(cam_=core, obj_=o))

    for o in range(4):
        mine = own_target & (obj == o)

        @pl.when(jnp.logical_not(mine))
        def _():
            sum_x(o).start()

        @pl.when(mine)
        def _():
            pltpu.make_async_copy(gxs.at[o], gxr.at[x], gx_r.at[x]).start()

    @pl.loop(pairs - 3, pairs)
    def _(i):
        finish(i)

    for o in range(4):
        pltpu.make_async_copy(gxs.at[o], gxr.at[o], gx_r.at[o]).wait()
    total = gxr[0].astype(F32) + gxr[1].astype(F32) + gxr[2].astype(F32) + gxr[3].astype(F32)
    gwo_ref[...] = total[0:10, :] * scale

    for t in range(4):
        @pl.when(jnp.logical_not(own_target & (x == t)))
        def _():
            w_to(t).wait_send()

        @pl.when(jnp.logical_not(own_target & (obj == t)))
        def _():
            sum_x(t).wait_send()

    for n in range(6):
        y_copy(n).wait_send()
        sum_y(n).wait_send()
    d_swap.wait_send()
    cross_own.wait_send()

    @pl.loop(0, RING)
    def _(h):
        up_copy(h, 0).wait_send()
        down_copy(h, 0).wait_send()
        for up in (True, False):
            cross(h, up).wait_send()
            cross(h, up, xh).wait_send()
        for sub in range(len(SUBS)):
            sum_up(h, sub).wait_send()
            sum_down(h, sub).wait_send()

    @pl.loop(0, pairs)
    def _(i):
        send_k(i).wait_send()
        send_v(i).wait_send()
        swap_att(i).wait_send()
        give_k(i).wait_send()
        give_v(i).wait_send()
        put_q(i).wait()
        put_k(i).wait()
        put_v(i).wait()


def body(queries, keys, values, d_out, w_out):
    shape = queries.shape
    width, model = queries.shape[4], d_out.shape[4]
    toks = queries.shape[1] * queries.shape[2] * queries.shape[3]
    tokens = toks * lax.axis_size("cam") * lax.axis_size("band") * lax.axis_size("obj")
    scale = float(tokens) ** -0.5
    pairs = width // 128
    cols = w_out.shape[1]
    blk = width // NZ
    dma = lambda *n: pltpu.SemaphoreType.DMA(n)
    flat = lambda a: a.reshape(toks, a.shape[4])
    any_ = pl.BlockSpec(memory_space=pl.ANY)
    vmem = pl.BlockSpec(memory_space=pltpu.VMEM)
    grad = jax.ShapeDtypeStruct((toks, width), BF)
    scratch = [
        pltpu.VMEM((pairs, toks, 128), BF),
        pltpu.VMEM((pairs, 2, toks, 128), BF),
        pltpu.VMEM((pairs, 2, toks, 128), BF),
        pltpu.VMEM((toks, model), BF),
        pltpu.VMEM((2 * toks, cols), BF),
        pltpu.VMEM((toks, cols), BF),
        pltpu.VMEM((16, cols), BF),
        pltpu.VMEM((4, 16, cols), BF),
        pltpu.VMEM((4, 48, cols), BF),
        pltpu.VMEM((width, cols), BF),
        pltpu.VMEM((width, cols), BF),
        pltpu.VMEM((width, 2 * toks), BF),
        pltpu.VMEM((pairs, 1, 2 * toks), F32),
        pltpu.VMEM((128, 2 * toks), F32),
        pltpu.VMEM((pairs, 2, toks, 128), BF),
        pltpu.VMEM((pairs, 2, toks, 128), BF),
        pltpu.VMEM((pairs, 2, toks, 128), F32),
        pltpu.VMEM((pairs, toks, 128), BF),
        pltpu.VMEM((pairs, toks, 128), BF),
        pltpu.VMEM((pairs, toks, 128), BF),
        pltpu.VMEM((blk, cols), F32),
        pltpu.VMEM((RING, 2, blk // 2, cols), BF),
        pltpu.VMEM((RING, 2, blk // 2, cols), BF),
        pltpu.VMEM((4, 48, cols), BF),
        pltpu.VMEM((4, 48, cols), BF),
        pltpu.VMEM((48, cols), BF),
        pltpu.VMEM((4, 16, cols), BF),
        pltpu.VMEM((4, 16, cols), BF),
        dma(pairs), dma(pairs), dma(pairs), pltpu.SemaphoreType.DMA,
        dma(4), dma(4), dma(6), dma(6), dma(RING), dma(RING), dma(RING), dma(RING),
        dma(2 * RING + 1), dma(2 * RING + 1), dma(2 * RING), dma(2 * RING), dma(pairs), dma(pairs), dma(pairs), dma(pairs),
        pltpu.SemaphoreType.DMA, pltpu.SemaphoreType.DMA, dma(pairs), dma(pairs),
        dma(pairs), dma(pairs), dma(pairs), dma(pairs),
        dma(RING, 2), dma(RING, 2), dma(RING, 2), dma(RING, 2), dma(6), dma(6), dma(4), dma(4),
        dma(pairs), dma(pairs), dma(pairs),
    ]
    gq, gk, gv, gwo = pl.pallas_call(
        functools.partial(kernel, scale),
        out_shape=(grad, grad, grad, jax.ShapeDtypeStruct(w_out.shape, F32)),
        in_specs=[any_] * 4 + [vmem],
        out_specs=(any_, any_, any_, vmem),
        scratch_shapes=scratch,
        compiler_params=pltpu.CompilerParams(
            collective_id=0, has_side_effects=True, vmem_limit_bytes=64 * 1024 * 1024 - 65536),
        name="row_attention_backward",
    )(flat(queries), flat(keys), flat(values), flat(d_out), w_out)
    return gq.reshape(shape), gk.reshape(shape), gv.reshape(shape), gwo


def solution(mesh):
    act = P("obj", "cam", "band", None, None)
    proj = P(("band", "obj"), "cam")
    return jax.shard_map(
        body,
        mesh=mesh,
        in_specs=(act, act, act, act, proj),
        out_specs=(act, act, act, proj),
        check_vma=False,
    )
```

```python
import functools
import math

import jax
import jax.numpy as jnp
from jax import lax
from jax.experimental import pallas as pl
from jax.experimental.pallas import tpu as pltpu
from jax.sharding import PartitionSpec as P

BF = jnp.bfloat16
F32 = jnp.float32
MESH = pl.DeviceIdType.MESH
NY, NZ = 4, 8
RING = NZ - 1
LAG = 6
RING_AT = 3
SUM_AT = 8
SHARED = 16
TOP, REST = pl.ds(0, 32), pl.ds(32, 16)
SUBS = ((0, 48), (48, 32))
EXP_SCALE = 0.125 / math.log(2.0)


def nn(a, b):
    return lax.dot_general(a, b, (((1,), (0,)), ((), ())), preferred_element_type=F32)


def nt(a, b):
    return lax.dot_general(a, b, (((1,), (1,)), ((), ())), preferred_element_type=F32)


def picker(rows, cols, row_step, col_step, width):
    r = lax.broadcasted_iota(jnp.int32, (rows, cols), 0)
    c = lax.broadcasted_iota(jnp.int32, (rows, cols), 1)
    pick = jnp.zeros((rows, cols), F32)
    for b in range(4):
        k = r - row_step * b
        hit = (k >= 0) & (k < width) & (c - col_step * b == k)
        pick = pick + jnp.where(hit, 1.0, 0.0).astype(F32)
    return pick.astype(BF)


def halves(x, axis):
    index = lax.broadcasted_iota(jnp.int32, x.shape, axis)
    first = jnp.where(index < x.shape[axis] // 2, x, 0.0)
    return first.astype(BF), (x - first).astype(BF)


def kernel(scale, q_hbm, k_hbm, v_hbm, d_hbm, w_ref, gq_hbm, gk_hbm, gv_hbm, gwo_ref,
           qb, kb, vb, dfull, dcat, doth, wpad, wx, wy, wown, woth, att, lse, osum,
           dks, dkr, dko, gq_st, gk_st, gv_st, gacc, rss, rsr, gys, gyr, gyf, gxs, gxr,
           q_ld, k_ld, v_ld, d_ld, wx_s, wx_r, wy_s, wy_r, zr_s, zr_r, zl_s, zl_r,
           oc_s, oc_r, wp_s, wp_r, k_s, k_r, v_s, v_r, dx_s, dx_r, at_s, at_r, dk_s, dk_r, dv_s, dv_r,
           rr_s, rr_r, rl_s, rl_r, gy_s, gy_r, gx_s, gx_r, gq_o, gk_o, gv_o):
    pairs, toks = qb.shape[0], qb.shape[1]
    cols = wpad.shape[1]
    blk = wown.shape[0] // NZ
    half = blk // 2
    cam, band, obj = lax.axis_index("cam"), lax.axis_index("band"), lax.axis_index("obj")
    z, y = band // NY, band % NY
    xh, core = obj // 2, obj % 2
    x = xh * 2 + cam
    base = (blk * z + half) // 128

    def dev(cam_=None, band_=None, obj_=None):
        return {
            "cam": cam if cam_ is None else cam_,
            "band": band if band_ is None else band_,
            "obj": obj if obj_ is None else obj_,
        }

    def at_z(shift):
        return dev(band_=lax.rem(z + shift + NZ, NZ) * NY + y)

    def at_y(shift):
        return dev(band_=z * NY + lax.rem(y + shift, NY))

    cam_peer = dev(cam_=1 - cam)
    wrap_peer = dev(cam_=1 - cam, obj_=(1 - xh) * 2 + core)
    core_peer = dev(obj_=xh * 2 + 1 - core)
    z_up, z_down = at_z(1), at_z(-1)
    y_up, y_down = at_y(1), at_y(NY - 1)

    def remote(src, dst, send, recv, device):
        return pltpu.make_async_remote_copy(
            src_ref=src, dst_ref=dst, send_sem=send, recv_sem=recv, device_id=device,
            device_id_type=MESH)

    def order(i):
        step = (i + 1) // 2
        sign = 2 * (i % 2) - 1
        return lax.rem(base + sign * step + pairs, pairs)

    def lanes(i):
        return pl.ds(pl.multiple_of(order(i) * 128, 128), 128)

    def load_q(i):
        return pltpu.make_async_copy(q_hbm.at[:, lanes(i)], qb.at[i], q_ld.at[i])

    def load_k(i):
        return pltpu.make_async_copy(k_hbm.at[:, lanes(i)], kb.at[i, 0], k_ld.at[i])

    def load_v(i):
        return pltpu.make_async_copy(v_hbm.at[:, lanes(i)], vb.at[i, 0], v_ld.at[i])

    def send_k(i):
        return remote(k_hbm.at[:, lanes(i)], kb.at[i, 1], k_s.at[i], k_r.at[i], cam_peer)

    def send_v(i):
        return remote(v_hbm.at[:, lanes(i)], vb.at[i, 1], v_s.at[i], v_r.at[i], cam_peer)

    load_d = pltpu.make_async_copy(d_hbm, dfull, d_ld)
    load_d.start()
    wpad[...] = jnp.zeros_like(wpad)
    wpad[0:10, :] = w_ref[...]

    @pl.loop(0, pairs)
    def _(i):
        load_q(i).start()
        load_k(i).start()
        load_v(i).start()

    barrier = pltpu.get_barrier_semaphore()
    peers = [dev(cam_=lax.rem(cam + a, 2), obj_=lax.rem(obj + b, 4))
             for a in range(2) for b in range(4) if a + b > 0]
    peers += [y_up, y_down, z_up, z_down]
    for peer in peers:
        pl.semaphore_signal(barrier, inc=1, device_id=peer, device_id_type=MESH)
    pl.semaphore_wait(barrier, len(peers))

    def w_to(t):
        return remote(wpad, wx.at[obj], wx_s.at[t], wx_r.at[obj],
                      dev(cam_=t % 2, obj_=(t // 2) * 2 + cam))

    own_target = core == cam
    for t in range(4):
        mine = own_target & (x == t)

        @pl.when(jnp.logical_not(mine))
        def _():
            w_to(t).start()

    @pl.when(own_target)
    def _():
        pltpu.make_async_copy(wpad, wx.at[obj], wx_r.at[obj]).start()

    @pl.loop(0, pairs)
    def _(i):
        send_k(i).start()
        send_v(i).start()

    join_x = picker(48, 64, 10, 16, 10)
    for o in range(4):
        pltpu.make_async_copy(wpad, wx.at[o], wx_r.at[o]).wait()
    joined = nn(join_x, wx[...].reshape(64, cols)).astype(BF)
    wy[y] = joined

    def y_copy(n):
        block = (y, y, y, y, lax.rem(y + NY - 1, NY), lax.rem(y + 1, NY))[n]
        rows = (TOP, REST, REST, TOP, TOP, REST)[n]
        return remote(wy.at[block, rows], wy.at[block, rows], wy_s.at[n], wy_r.at[n],
                      y_down if n % 2 else y_up)

    for n in range(4):
        y_copy(n).start()

    load_d.wait()
    low, high = dfull[:, 0:cols], dfull[:, cols:2 * cols]

    @pl.when(core == 0)
    def _():
        dcat[0:toks, :] = low
        doth[...] = high

    @pl.when(core == 1)
    def _():
        dcat[0:toks, :] = high
        doth[...] = low

    d_swap = remote(doth, dcat.at[pl.ds(toks, toks)], dx_s, dx_r, core_peer)
    d_swap.start()

    join_y = picker(blk, 4 * 48, 40, 48, 40)
    for n in range(2):
        y_copy(n).wait_recv()
        y_copy(n + 4).start()
    for n in range(2, 6):
        y_copy(n).wait_recv()

    def block_rows(b, size=None, off=0):
        return pl.ds(pl.multiple_of(b * blk + off, 16), blk if size is None else size)

    wown[block_rows(z), :] = nn(join_y, wy[...].reshape(4 * 48, cols)).astype(BF)

    def up_copy(h, back):
        b = lax.rem(z - h // 2 - back + NZ, NZ)
        rows = block_rows(b, half - SHARED, (h % 2) * half + SHARED * xh)
        return remote(wown.at[rows], wown.at[rows], zr_s.at[h], zr_r.at[h], z_up)

    def down_copy(h, back):
        b = lax.rem(z + h // 2 + back, NZ)
        rows = block_rows(b, half - SHARED, (1 - h % 2) * half + SHARED * xh)
        return remote(wown.at[rows], wown.at[rows], zl_s.at[h], zl_r.at[h], z_down)

    def cross(h, up, kind=None):
        b = lax.rem(z - h // 2 - 1 + NZ, NZ) if up else lax.rem(z + h // 2 + 1, NZ)
        j = h % 2 if up else 1 - h % 2
        n = 2 * h + (0 if up else 1)
        if kind is not None:
            rows = block_rows(b, SHARED, j * half + (half - SHARED) * kind)
            return remote(wown.at[rows], wown.at[rows], wp_s.at[n], wp_r.at[n], wrap_peer)
        rows = block_rows(b, half, j * half)
        return remote(wown.at[rows], woth.at[rows], oc_s.at[n], oc_r.at[n], core_peer)

    own_rows = block_rows(z)
    cross_own = remote(wown.at[own_rows], woth.at[own_rows], oc_s.at[2 * RING], oc_r.at[2 * RING], core_peer)
    for h in range(2):
        up_copy(h, 0).start()
        down_copy(h, 0).start()
    cross_own.start()

    def ring(h):
        up_copy(h, 1).wait_recv()

        @pl.when(h + 2 < RING)
        def _():
            up_copy(h + 2, 0).start()

        cross(h, True, xh).start()

    def ring_down(h):
        down_copy(h, 1).wait_recv()

        @pl.when(h + 2 < RING)
        def _():
            down_copy(h + 2, 0).start()

        cross(h, False, xh).start()

    def split_q(i):
        first, second = halves(qb[i].astype(F32), 1)
        return jnp.concatenate([first, second], axis=0)

    def swap_att(i):
        rows = pl.ds(pl.multiple_of(order(i) * 128, 128), 128)
        return remote(att.at[rows, pl.ds(0, toks)], att.at[rows, pl.ds(toks, toks)],
                      at_s.at[i], at_r.at[i], core_peer)

    part = 2 * toks // 3

    def forward(i):
        load_q(i).wait()
        load_k(i).wait()
        load_v(i).wait()
        send_k(i).wait_recv()
        send_v(i).wait_recv()
        kk = kb[i].reshape(2 * toks, 128)
        vt = vb[i].reshape(2 * toks, 128).T
        qm = split_q(i)
        for n in range(3):
            s = nt(kk, qm[n * part:(n + 1) * part])
            top = jnp.max(s, axis=0, keepdims=True)
            e = jnp.exp2((s - top) * EXP_SCALE)
            total = jnp.sum(e, axis=0, keepdims=True)
            osum[:, n * part:(n + 1) * part] = nn(vt, e.astype(BF)) * (1.0 / total)
            lse[i, :, n * part:(n + 1) * part] = top * EXP_SCALE + jnp.log2(total)
        rows = pl.ds(pl.multiple_of(order(i) * 128, 128), 128)
        both = jnp.concatenate([osum[0:64, 0:toks], osum[64:128, toks:2 * toks]], axis=0)
        att[rows, 0:toks] = both.astype(BF)
        swap_att(i).start()

    def give_k(i):
        return remote(dks.at[i, 0], dkr.at[i, 0], dk_s.at[i], dk_r.at[i], cam_peer)

    def give_v(i):
        return remote(dks.at[i, 1], dkr.at[i, 1], dv_s.at[i], dv_r.at[i], cam_peer)

    def put_q(i):
        return pltpu.make_async_copy(gq_st.at[i], gq_hbm.at[:, lanes(i)], gq_o.at[i])

    def put_k(i):
        return pltpu.make_async_copy(gk_st.at[i], gk_hbm.at[:, lanes(i)], gk_o.at[i])

    def put_v(i):
        return pltpu.make_async_copy(gv_st.at[i], gv_hbm.at[:, lanes(i)], gv_o.at[i])

    def backward(i):
        rows = pl.ds(pl.multiple_of(order(i) * 128, 128), 128)
        da = nt(wown[rows, :], dcat[0:toks, :]) + nt(woth[rows, :], doth[...])
        da = da.astype(BF).astype(F32)
        prod = da * att[rows, 0:toks].astype(F32)
        delta = jnp.concatenate([jnp.sum(prod[0:64], axis=0, keepdims=True),
                                 jnp.sum(prod[64:128], axis=0, keepdims=True)], axis=1)
        dm = jnp.concatenate(halves(da, 0), axis=1)
        kk = kb[i].reshape(2 * toks, 128)
        vv = vb[i].reshape(2 * toks, 128)
        kt = kk.T
        qm = split_q(i)
        dk = dv = None
        for n in range(3):
            at = slice(n * part, (n + 1) * part)
            s = nt(kk, qm[at])
            p = jnp.exp2(s * EXP_SCALE - lse[i, :, at])
            dp = nn(vv, dm[:, at])
            ds = (p * (dp - delta[:, at])).astype(BF)
            dv_n = nt(p.astype(BF), dm[:, at])
            dk_n = nn(ds, qm[at])
            dv = dv_n if dv is None else dv + dv_n
            dk = dk_n if dk is None else dk + dk_n
            osum[:, at] = nn(kt, ds)
        dk = dk * 0.125
        dks[i, 0] = dk[toks:].astype(BF)
        dks[i, 1] = dv[toks:].astype(BF)
        give_k(i).start()
        give_v(i).start()
        dko[i, 0] = dk[:toks]
        dko[i, 1] = dv[:toks]
        both = jnp.concatenate([osum[0:64, 0:toks], osum[64:128, toks:2 * toks]], axis=0)
        gq_st[i] = (both.T * 0.125).astype(BF)
        put_q(i).start()

    def finish(i):
        give_k(i).wait_recv()
        gk_st[i] = (dko[i, 0] + dkr[i, 0].astype(F32)).astype(BF)
        put_k(i).start()
        give_v(i).wait_recv()
        gv_st[i] = (dko[i, 1] + dkr[i, 1].astype(F32)).astype(BF)
        put_v(i).start()

    def sum_up(s, sub):
        at = pl.ds(*SUBS[sub])
        return remote(rss.at[s, 0, at], rsr.at[s, 0, at], rr_s.at[s, sub], rr_r.at[s, sub], z_up)

    def sum_down(s, sub):
        at = pl.ds(*SUBS[sub])
        return remote(rss.at[s, 1, at], rsr.at[s, 1, at], rl_s.at[s, sub], rl_r.at[s, sub], z_down)

    def own_term(s):
        owner_up = lax.rem(z - 1 - s + 2 * NZ, NZ)
        owner_down = lax.rem(z + 1 + s, NZ)
        rows = jnp.concatenate([att[block_rows(owner_up, half), :],
                                att[block_rows(owner_down, half, half), :]], axis=0)
        gacc[...] = nn(rows, dcat[...])

    def sum_step(s, sub):
        off, size = SUBS[sub]
        for way, copy in enumerate((sum_up, sum_down)):
            at = slice(way * half + off, way * half + off + size)

            @pl.when(s > 0)
            def _():
                copy(s - 1, sub).wait_recv()
                gacc[at, :] = gacc[at, :] + rsr[s - 1, way, off:off + size].astype(F32)

            @pl.when(s < RING)
            def _():
                rss[s, way, off:off + size] = gacc[at, :].astype(BF)
                copy(s, sub).start()

    @pl.loop(0, max(LAG + pairs, SUM_AT + NZ))
    def _(t):
        s = t - SUM_AT

        @pl.when(s == 0)
        def _():
            d_swap.wait_recv()
            own_term(0)

        @pl.when((s >= 0) & (s < NZ))
        def _():
            sum_step(s, 0)

        h = t - RING_AT

        @pl.when((h >= 0) & (h < RING))
        def _():
            ring(h)

        @pl.when(t < pairs)
        def _():
            forward(t)

        @pl.when(h == 0)
        def _():
            cross_own.wait_recv()

        @pl.when((h >= 2) & (h <= RING + 1))
        def _():
            cross(h - 2, True).wait_recv()
            cross(h - 2, False).wait_recv()

        @pl.when((h >= 1) & (h <= RING))
        def _():
            for up in (True, False):
                cross(h - 1, up, 1 - xh).wait_recv()
                cross(h - 1, up).start()

        @pl.when((h >= 0) & (h < RING))
        def _():
            ring_down(h)

        @pl.when((t >= 1) & (t < pairs))
        def _():
            swap_att(t - 1).wait_recv()

        @pl.when(t == pairs - 1)
        def _():
            swap_att(t).wait_recv()

        @pl.when((t >= LAG) & (t < LAG + pairs))
        def _():
            backward(t - LAG)

        @pl.when((s >= 0) & (s < NZ))
        def _():
            sum_step(s, 1)

        @pl.when((s >= 0) & (s < RING))
        def _():
            own_term(s + 1)

    y_next, y_last = lax.rem(y + 1, NY), lax.rem(y + NY - 1, NY)
    y_far = lax.rem(y + 2, NY)

    def sum_y(n):
        rows = (TOP, REST, REST, TOP, TOP, REST)[n]
        src = (gys.at[y_far], gys.at[y_far], gys.at[y_next], gys.at[y_last], gyf, gyf)[n]
        dst = (0, 1, 2, 3, 2, 3)[n]
        return remote(src.at[rows], gyr.at[dst, rows], gy_s.at[n], gy_r.at[n],
                      y_down if n % 2 else y_up)

    gys[...] = nn(picker(4 * 48, blk, 48, 40, 40), gacc[...].astype(BF)).astype(BF).reshape(4, 48, cols)
    for n in range(4):
        sum_y(n).start()

    @pl.loop(0, pairs - 6)
    def _(i):
        finish(i)

    sum_y(0).wait_recv()
    gyf[0:32] = (gys[y_next, 0:32].astype(F32) + gyr[0, 0:32].astype(F32)).astype(BF)
    sum_y(4).start()
    sum_y(1).wait_recv()
    gyf[32:48] = (gys[y_last, 32:48].astype(F32) + gyr[1, 32:48].astype(F32)).astype(BF)
    sum_y(5).start()

    @pl.loop(pairs - 6, pairs - 3)
    def _(i):
        finish(i)

    for n in range(2, 6):
        sum_y(n).wait_recv()
    summed = gys[y].astype(F32) + gyr[2].astype(F32) + gyr[3].astype(F32)
    gxs[...] = nn(picker(64, 48, 16, 10, 10), summed.astype(BF)).astype(BF).reshape(4, 16, cols)

    def sum_x(o):
        return remote(gxs.at[o], gxr.at[x], gx_s.at[o], gx_r.at[x], dev(cam_=core, obj_=o))

    for o in range(4):
        mine = own_target & (obj == o)

        @pl.when(jnp.logical_not(mine))
        def _():
            sum_x(o).start()

        @pl.when(mine)
        def _():
            pltpu.make_async_copy(gxs.at[o], gxr.at[x], gx_r.at[x]).start()

    @pl.loop(pairs - 3, pairs)
    def _(i):
        finish(i)

    for o in range(4):
        pltpu.make_async_copy(gxs.at[o], gxr.at[o], gx_r.at[o]).wait()
    total = gxr[0].astype(F32) + gxr[1].astype(F32) + gxr[2].astype(F32) + gxr[3].astype(F32)
    gwo_ref[...] = total[0:10, :] * scale

    for t in range(4):
        @pl.when(jnp.logical_not(own_target & (x == t)))
        def _():
            w_to(t).wait_send()

        @pl.when(jnp.logical_not(own_target & (obj == t)))
        def _():
            sum_x(t).wait_send()

    for n in range(6):
        y_copy(n).wait_send()
        sum_y(n).wait_send()
    d_swap.wait_send()
    cross_own.wait_send()

    @pl.loop(0, RING)
    def _(h):
        up_copy(h, 0).wait_send()
        down_copy(h, 0).wait_send()
        for up in (True, False):
            cross(h, up).wait_send()
            cross(h, up, xh).wait_send()
        for sub in range(len(SUBS)):
            sum_up(h, sub).wait_send()
            sum_down(h, sub).wait_send()

    @pl.loop(0, pairs)
    def _(i):
        send_k(i).wait_send()
        send_v(i).wait_send()
        swap_att(i).wait_send()
        give_k(i).wait_send()
        give_v(i).wait_send()
        put_q(i).wait()
        put_k(i).wait()
        put_v(i).wait()


def body(queries, keys, values, d_out, w_out):
    shape = queries.shape
    width, model = queries.shape[4], d_out.shape[4]
    toks = queries.shape[1] * queries.shape[2] * queries.shape[3]
    tokens = toks * lax.axis_size("cam") * lax.axis_size("band") * lax.axis_size("obj")
    scale = float(tokens) ** -0.5
    pairs = width // 128
    cols = w_out.shape[1]
    blk = width // NZ
    dma = lambda *n: pltpu.SemaphoreType.DMA(n)
    flat = lambda a: a.reshape(toks, a.shape[4])
    any_ = pl.BlockSpec(memory_space=pl.ANY)
    vmem = pl.BlockSpec(memory_space=pltpu.VMEM)
    grad = jax.ShapeDtypeStruct((toks, width), BF)
    scratch = [
        pltpu.VMEM((pairs, toks, 128), BF),
        pltpu.VMEM((pairs, 2, toks, 128), BF),
        pltpu.VMEM((pairs, 2, toks, 128), BF),
        pltpu.VMEM((toks, model), BF),
        pltpu.VMEM((2 * toks, cols), BF),
        pltpu.VMEM((toks, cols), BF),
        pltpu.VMEM((16, cols), BF),
        pltpu.VMEM((4, 16, cols), BF),
        pltpu.VMEM((4, 48, cols), BF),
        pltpu.VMEM((width, cols), BF),
        pltpu.VMEM((width, cols), BF),
        pltpu.VMEM((width, 2 * toks), BF),
        pltpu.VMEM((pairs, 1, 2 * toks), F32),
        pltpu.VMEM((128, 2 * toks), F32),
        pltpu.VMEM((pairs, 2, toks, 128), BF),
        pltpu.VMEM((pairs, 2, toks, 128), BF),
        pltpu.VMEM((pairs, 2, toks, 128), F32),
        pltpu.VMEM((pairs, toks, 128), BF),
        pltpu.VMEM((pairs, toks, 128), BF),
        pltpu.VMEM((pairs, toks, 128), BF),
        pltpu.VMEM((blk, cols), F32),
        pltpu.VMEM((RING, 2, blk // 2, cols), BF),
        pltpu.VMEM((RING, 2, blk // 2, cols), BF),
        pltpu.VMEM((4, 48, cols), BF),
        pltpu.VMEM((4, 48, cols), BF),
        pltpu.VMEM((48, cols), BF),
        pltpu.VMEM((4, 16, cols), BF),
        pltpu.VMEM((4, 16, cols), BF),
        dma(pairs), dma(pairs), dma(pairs), pltpu.SemaphoreType.DMA,
        dma(4), dma(4), dma(6), dma(6), dma(RING), dma(RING), dma(RING), dma(RING),
        dma(2 * RING + 1), dma(2 * RING + 1), dma(2 * RING), dma(2 * RING), dma(pairs), dma(pairs), dma(pairs), dma(pairs),
        pltpu.SemaphoreType.DMA, pltpu.SemaphoreType.DMA, dma(pairs), dma(pairs),
        dma(pairs), dma(pairs), dma(pairs), dma(pairs),
        dma(RING, 2), dma(RING, 2), dma(RING, 2), dma(RING, 2), dma(6), dma(6), dma(4), dma(4),
        dma(pairs), dma(pairs), dma(pairs),
    ]
    gq, gk, gv, gwo = pl.pallas_call(
        functools.partial(kernel, scale),
        out_shape=(grad, grad, grad, jax.ShapeDtypeStruct(w_out.shape, F32)),
        in_specs=[any_] * 4 + [vmem],
        out_specs=(any_, any_, any_, vmem),
        scratch_shapes=scratch,
        compiler_params=pltpu.CompilerParams(
            collective_id=0, has_side_effects=True, vmem_limit_bytes=64 * 1024 * 1024 - 65536),
        name="row_attention_backward",
    )(flat(queries), flat(keys), flat(values), flat(d_out), w_out)
    return gq.reshape(shape), gk.reshape(shape), gv.reshape(shape), gwo


def solution(mesh):
    act = P("obj", "cam", "band", None, None)
    proj = P(("band", "obj"), "cam")
    return jax.shard_map(
        body,
        mesh=mesh,
        in_specs=(act, act, act, act, proj),
        out_specs=(act, act, act, proj),
        check_vma=False,
    )
```
